256 devices in a mesh: cuts: 32 (over y_lo, z, core), chan: 8 (over y_hi, x).
Axes of the slice: x: 4, y: 4 (y_hi: 2, y_lo: 2; y = y_hi * 2 + y_lo), z: 8, core: 2. Of those that a mesh axis runs over, the one named last changes fastest.
Arguments:
- data: bfloat16 [256, 384, 1024], P('cuts', None, 'chan'), may hold values from -6 to 6
- order: int32 [256], P('cuts'), may hold values from 0 to 255, as said below
- chan_factor: bfloat16 [1024, 64], P('chan'), may hold values from -0.1875 to 0.1875
- slice_weights: float32 [256, 64], P('cuts'), may hold values from 0.5 to 2
- smooth_aux: float32 [256, 384, 64], P('cuts', 'chan'), may hold values from -6 to 6
- coupled: float32 [256, 384, 64], P('cuts', 'chan'), may hold values from -6 to 6
- smooth_dual: float32 [256, 384, 64], P('cuts', 'chan'), may hold values from -2 to 2
- coupling_dual: float32 [256, 384, 64], P('cuts', 'chan'), may hold values from -2 to 2
- delta: float32 [64, 64], replicated, may hold values from -0.1125 to 1.1125, as said below
Outputs:
- evolving: float32 [256, 384, 64], P('cuts', 'chan')
- coupled_out: float32 [256, 384, 64], P('cuts', 'chan')
- delta_out: float32 [64, 64], replicated
The draws below stay inside these ranges and needn't reach their ends.
Inputs may be any that keep to these rules, and one draw needn't show every extreme that they name: `order`: within each aligned block of 8 entries (the slices of one index of cuts) the entries are a permutation of that block's own slice indices; entry k names the stored slice of phase bin k. `delta`: A full-rank matrix.
All inputs are finite; a program needn't handle non-finite values.
Results may differ from the reference program's by a relative error of at most 0.0003.
Values sent between devices are 32-bit elements; how exact they have to be, the bound alone decides.
A program may use at most 64 MiB of HBM per device.

```python
import math
import jax
import jax.numpy as jnp
from jax import lax

SLICE_DEV = 8
ROWS = 384
CHANNELS = 1024
RANK = 64
INNER = 3
SWEEPS = 4
POLAR = 8
SLICES = 256


def draw_order(key, part):
    blocks = SLICES // SLICE_DEV
    block_keys = jax.random.split(key, blocks)
    shuffled = jax.vmap(lambda sub_key: jax.random.permutation(sub_key, SLICE_DEV))(block_keys)
    offsets = jnp.arange(blocks, dtype=jnp.int32)[:, None] * SLICE_DEV
    return (shuffled.astype(jnp.int32) + offsets).reshape(SLICES)


def draw_delta(key, part):
    noise = jax.random.truncated_normal(key, -3.0, 3.0, (RANK, RANK), jnp.float32)
    return jnp.eye(RANK, dtype=jnp.float32) + 0.3 * RANK ** (-0.5) * noise


def shard_levels(rng, shape, shards, least, largest):
    level, own = 1.0, jax.random.fold_in(rng, 6)
    for axis_at, parts in shards:
        steps = jnp.exp(jax.random.uniform(jax.random.fold_in(own, axis_at), (parts,), jnp.float32, least / len(shards), largest / len(shards)))
        level = level * jnp.repeat(steps, shape[axis_at] // parts).reshape([-1 if axis == axis_at else 1 for axis in range(len(shape))])
    return level


def centred(rng, dims, scale, reach, cuts=(), kind=jnp.bfloat16):
    entries = jax.random.normal(rng, dims, jnp.float32) * scale
    if len(cuts) > 0:
        entries = shard_levels(rng, dims, cuts, -0.22, 0.18) * entries
    return jnp.clip(entries, min=-reach, max=reach).astype(kind)


def setup_inputs(seed: int = 0) -> dict:
    key_of = jax.random.split(jax.random.key(seed), 10)
    data = centred(key_of[0], (SLICES, ROWS, CHANNELS), 1.0, 6.0, ((0, 32), (2, 8)))
    order = draw_order(jax.random.fold_in(key_of[9], 71), 0)
    chan_factor = centred(key_of[2], (CHANNELS, RANK), CHANNELS ** -0.5, 0.1875, ((0, 8),))
    slice_weights = jnp.clip(jnp.exp(math.log(2.0) - 1.3862944 * jax.random.uniform(key_of[3], (SLICES, RANK), jnp.float32) ** shard_levels(key_of[3], (SLICES, RANK), ((0, 32),), -0.2, 0.2)), 0.5, 2.0)
    smooth_aux = centred(key_of[4], (SLICES, ROWS, RANK), 1.0, 6.0, ((0, 32), (1, 8)), jnp.float32)
    coupled = centred(key_of[5], (SLICES, ROWS, RANK), 1.0, 6.0, ((0, 32), (1, 8)), jnp.float32)
    smooth_dual = centred(key_of[6], (SLICES, ROWS, RANK), 0.3, 2.0, ((0, 32), (1, 8)), jnp.float32)
    coupling_dual = centred(key_of[7], (SLICES, ROWS, RANK), 0.3, 2.0, ((0, 32), (1, 8)), jnp.float32)
    delta = draw_delta(jax.random.fold_in(key_of[9], 71), 0)
    return dict(data=data, order=order, chan_factor=chan_factor, slice_weights=slice_weights, smooth_aux=smooth_aux, coupled=coupled, smooth_dual=smooth_dual, coupling_dual=coupling_dual, delta=delta)


smooth_weight = 1.0
eps_trace = 1e-06
highest = lax.Precision.HIGHEST

def setup_system(slice_weights, factor_gram):
    rank = factor_gram.shape[0]
    identity = jnp.eye(rank, dtype=jnp.float32)
    diagonal_gram = jnp.diagonal(factor_gram)
    rho = lax.optimization_barrier(jnp.sum(slice_weights * slice_weights * diagonal_gram[None, :], axis=1)) / rank
    system = slice_weights[:, :, None] * factor_gram[None] * slice_weights[:, None, :]
    system = system + 2.0 * rho[:, None, None] * identity
    factors = jax.vmap(jnp.linalg.cholesky)(system)
    inverse = jax.vmap(lambda lower: jax.scipy.linalg.cho_solve((lower, True), identity))(factors)
    return (rho, inverse)

def polar_terms(gram, delta_now):
    rank = gram.shape[1]
    identity = jnp.eye(rank, dtype=jnp.float32)
    left = jnp.einsum('rs,kst->krt', delta_now, gram, precision=highest)
    normal = jnp.einsum('krt,ut->kru', left, delta_now, precision=highest)
    trace = jnp.trace(normal, axis1=1, axis2=2) + eps_trace
    current = normal / trace[:, None, None]
    root = jnp.broadcast_to(identity, normal.shape)
    for step in range(POLAR):
        bracket = 1.5 * identity - 0.5 * jnp.einsum('krs,kst->krt', root, current, precision=highest)
        current = jnp.einsum('krs,kst->krt', current, bracket, precision=highest)
        root = jnp.einsum('krs,kst->krt', bracket, root, precision=highest)
    scale = 1.0 / jnp.sqrt(trace)
    partial_value = jnp.einsum('ksr,st->krt', root, delta_now, precision=highest)
    partial_value = jnp.einsum('krt,ktu->kru', partial_value, gram, precision=highest) * scale[:, None, None]
    return (root, scale, partial_value)

def coupled_update(tall, root, scale, delta_now, delta_new):
    mixer = jnp.einsum('sr,kst->krt', delta_now, root, precision=highest)
    mixer = jnp.einsum('krt,tu->kru', mixer, delta_new, precision=highest) * scale[:, None, None]
    return jnp.einsum('kir,kru->kiu', tall, mixer, precision=highest)

def reference(data, order, chan_factor, slice_weights, smooth_aux, coupled, smooth_dual, coupling_dual, delta):
    flat = data.reshape(SLICES * ROWS, CHANNELS)
    projected = jnp.dot(flat.astype(jnp.float32), chan_factor.astype(jnp.float32), preferred_element_type=jnp.float32).reshape(SLICES, ROWS, RANK)
    projected = jnp.take(projected, order, axis=0)
    factor_gram = jnp.dot(chan_factor.T.astype(jnp.float32), chan_factor.astype(jnp.float32), preferred_element_type=jnp.float32)
    rho, inverse = setup_system(slice_weights, factor_gram)
    data_side = projected * slice_weights[:, None, :]
    rho_cols = rho[:, None, None]
    aux = smooth_aux
    coup = coupled
    dual_s = smooth_dual
    dual_c = coupling_dual
    delta_now = delta
    evolving = aux
    for inner in range(INNER):
        rhs = data_side + rho_cols * (aux - dual_s + coup - dual_c)
        evolving = jnp.einsum('kir,krs->kis', rhs, inverse, precision=highest)
        target = evolving + dual_s
        for sweep in range(SWEEPS):
            beside = jnp.roll(aux, 1, 0) + jnp.roll(aux, -1, 0)
            aux = (rho_cols * target + 2.0 * smooth_weight * beside) / (rho_cols + 4.0 * smooth_weight)
        tall = evolving + dual_c
        gram = jnp.einsum('kir,kis->krs', tall, tall, precision=highest)
        root, scale, partial_value = polar_terms(gram, delta_now)
        delta_new = lax.optimization_barrier(jnp.sum(partial_value, axis=0)) / SLICES
        coup = coupled_update(tall, root, scale, delta_now, delta_new)
        dual_s = dual_s + evolving - aux
        dual_c = dual_c + evolving - coup
        delta_now = delta_new
    return (evolving, coup, delta_now)
```

```python
import jax
import jax.numpy as jnp
from jax import lax
from jax.experimental import pallas as pl
from jax.experimental.pallas import tpu as pltpu
from jax.sharding import PartitionSpec as P

INNER = 3
POLAR = 8
NEWTON = 7
EPS_TRACE = 1e-06
F32 = jnp.float32
HIGH = lax.Precision.HIGHEST
MESH = pl.DeviceIdType.MESH
CHEB_A = 0.1328125 / 1.2578125
CHEB_B = -1.0 / (512.0 * 1.2578125)


def mm(a, b):
    return jnp.dot(a, b, precision=HIGH, preferred_element_type=F32)


def mm_tn(a, b):
    return lax.dot_general(a, b, (((0,), (0,)), ((), ())), precision=HIGH, preferred_element_type=F32)


def kernel(
    order, data_h, fac_h, w_h, aux_h, coup_h, ds_h, dc_h, delta_h,
    evo_o, coup_o, delta_o,
    data_v, fac_v, w_v, aux_v, coup_v, ds_v, dc_v, delta_v,
    psend, precv, ysend, yrecv, fg, x2, cr, left_s, k2_s,
    gsend, grecv, gall, qsend, qrecv, zbuf, qall,
    aux_p, dss, dcs, talls, evos, at_s, baux, hal_a, hal_t, bsend, hal_b,
    load_sem, px_s, px_r, py_s, py_r, fg_s, fg_r,
    g1_s, g1_r, g2_s, g2_r, q1_s, q1_r, z_s, z_r, q2_s, q2_r, ha_s, ha_r, ht_s, ht_r, hb_s, hb_r,
):
    cuts = lax.axis_index("cuts")
    chan = lax.axis_index("chan")
    core = lax.rem(cuts, 2)
    zz = lax.rem(cuts // 2, 8)
    ylo = cuts // 16
    quad = ylo * 2 + core
    xx = lax.rem(chan, 4)
    yhi = chan // 4
    left_id = lax.rem(cuts + 31, 32)
    right_id = lax.rem(cuts + 1, 32)

    def z_dev(z):
        return (ylo * 16 + z * 2 + core, chan)

    def quad_dev(q):
        return ((q // 2) * 16 + zz * 2 + lax.rem(q, 2), chan)

    sent = []

    def send(src, dst, ssem, rsem, dev):
        copy = pltpu.make_async_remote_copy(
            src_ref=src, dst_ref=dst, send_sem=ssem, recv_sem=rsem, device_id=dev, device_id_type=MESH
        )
        copy.start()
        sent.append(copy)

    def arrived(dst, ssem, rsem):
        pltpu.make_async_remote_copy(
            src_ref=dst, dst_ref=dst, send_sem=ssem, recv_sem=rsem, device_id=(left_id, chan), device_id_type=MESH
        ).wait_recv()

    loads = []
    for n, (src, dst) in enumerate(
        (
            (fac_h, fac_v), (data_h, data_v), (w_h, w_v), (aux_h, aux_v), (coup_h, coup_v),
            (ds_h, ds_v), (dc_h, dc_v), (delta_h, delta_v),
        )
    ):
        copy = pltpu.make_async_copy(src, dst, load_sem.at[n])
        copy.start()
        loads.append(copy)

    barrier = pltpu.get_barrier_semaphore()
    greet = [(cuts, lax.rem(chan + d, 8)) for d in range(1, 8)]
    greet += [z_dev(lax.rem(zz + d, 8)) for d in range(1, 8)]
    greet += [quad_dev(lax.rem(quad + d, 4)) for d in range(1, 4)]
    greet += [(left_id, chan), (right_id, chan)]
    for dev in greet:
        pl.semaphore_signal(barrier, inc=1, device_id=dev, device_id_type=MESH)

    lane = lax.broadcasted_iota(jnp.int32, (1, 128), 1)
    low = lane < 64
    row_i = lax.broadcasted_iota(jnp.int32, (128, 128), 0)
    col_i = lax.broadcasted_iota(jnp.int32, (128, 128), 1)
    eye_b = row_i == col_i
    eye = eye_b.astype(F32)

    def swap(v):
        return pltpu.roll(v, 64, 1)

    def unpack2(g, h):
        a = jnp.concatenate([g, swap(g)], axis=0)
        b = jnp.concatenate([swap(h), h], axis=0)
        zero = jnp.zeros_like(a)
        return jnp.concatenate([jnp.where(low, a, zero), jnp.where(low, zero, b)], axis=0)

    def pack2(t):
        g = jnp.where(low, t[0:32], swap(t[32:64]))
        h = jnp.where(low, swap(t[64:96]), t[96:128])
        return g, h

    def half_sums(v):
        zero = jnp.zeros_like(v)
        lo = jnp.sum(jnp.where(low, v, zero), axis=1, keepdims=True)
        hi = jnp.sum(jnp.where(low, zero, v), axis=1, keepdims=True)
        return jnp.where(low, lo, hi)

    loads[0].wait()
    fac = fac_v[...]
    partial_gram = lax.dot_general(fac, fac, (((0,), (0,)), ((), ())), preferred_element_type=F32)
    fg[chan] = jnp.concatenate([partial_gram[0:32], partial_gram[32:64]], axis=1)
    pl.semaphore_wait(barrier, len(greet))
    for d in range(1, 8):
        peer = lax.rem(chan + d, 8)
        send(fg.at[chan], fg.at[chan], fg_s.at[d - 1], fg_r.at[chan], (cuts, peer))

    zero_fac = jnp.zeros_like(fac)
    fac2 = jnp.concatenate(
        [jnp.concatenate([fac, zero_fac], axis=1), jnp.concatenate([zero_fac, fac], axis=1)], axis=0
    )
    loads[1].wait()
    for j in range(4):
        first = data_v[lax.rem(order[j], 8)]
        second = data_v[lax.rem(order[j + 4], 8)]
        out = jnp.dot(jnp.concatenate([first, second], axis=1), fac2, preferred_element_type=F32)
        for c in range(8):
            psend[c % 4, c // 4, j] = out[48 * c : 48 * c + 48]
    for d in (2, 1, 3):
        to = lax.rem(xx + d, 4)
        send(psend.at[to], precv.at[xx], px_s.at[d - 1], px_r.at[xx], (cuts, yhi * 4 + to))

    for n in range(2, 8):
        loads[n].wait()
    for j in range(4):
        aux_p[0, j] = jnp.concatenate([aux_v[j], aux_v[j + 4]], axis=1)
        dss[j] = jnp.concatenate([ds_v[j], ds_v[j + 4]], axis=1)
        dcs[j] = jnp.concatenate([dc_v[j], dc_v[j + 4]], axis=1)
        talls[j] = jnp.concatenate([coup_v[j], coup_v[j + 4]], axis=1)

    def halo_send(src, dst, ssem, rsem):
        send(src, dst.at[0], ssem.at[0], rsem.at[0], (right_id, chan))
        send(src, dst.at[1], ssem.at[1], rsem.at[1], (left_id, chan))

    halo_send(aux_p.at[0], hal_a.at[0], ha_s.at[0], ha_r.at[0])

    for d in range(1, 8):
        peer = lax.rem(chan + d, 8)
        arrived(fg.at[peer], fg_s.at[0], fg_r.at[peer])
    gram_sum = fg[0]
    for c in range(1, 8):
        gram_sum = gram_sum + fg[c]
    gram2 = unpack2(gram_sum, gram_sum)
    w = w_v[...]
    w2 = jnp.concatenate([w[0:4], w[4:8]], axis=1)
    diag_row = jnp.sum(jnp.where(eye_b, gram2, 0.0), axis=0, keepdims=True)
    rho = half_sums(w2 * w2 * diag_row) * (1.0 / 64.0)
    w_over = w2 / rho
    b_rows = 2.0 / (rho + 4.0)
    a_rows = rho / (rho + 4.0)
    bsend[0:4] = b_rows
    bsend[4:8] = b_rows
    halo_send(bsend, hal_b, hb_s, hb_r)
    systems = []
    for j in range(4):
        w_row = w2[j : j + 1]
        w_col = jnp.sum(jnp.where(eye_b, w_row, 0.0), axis=1, keepdims=True)
        system = gram2 * w_col * w_over[j : j + 1] + 2.0 * eye
        left_s[j] = system
        x2[j] = CHEB_A * eye + CHEB_B * system

    def newton(step, carry):
        for j in range(4):
            x = x2[j]
            x2[j] = mm(x, 2.0 * eye - mm(left_s[j], x))
        return carry

    lax.fori_loop(0, NEWTON, newton, 0)

    for d in range(1, 4):
        frm = lax.rem(xx + d, 4)
        arrived(precv.at[frm], px_s.at[0], px_r.at[frm])
    for j in range(4):
        total = psend[xx, 1 - yhi, j]
        for d in range(1, 4):
            total = total + precv[lax.rem(xx + d, 4), 1 - yhi, j]
        ysend[j] = total
    send(ysend, yrecv, py_s, py_r, (cuts, (1 - yhi) * 4 + xx))
    for j in range(4):
        total = psend[xx, yhi, j]
        for d in range(1, 4):
            total = total + precv[lax.rem(xx + d, 4), yhi, j]
        baux[j] = total
    arrived(yrecv, py_s, py_r)
    for j in range(4):
        baux[j] = (baux[j] + yrecv[j]) * w_over[j : j + 1]

    delta_in = delta_v[...]
    zero_d = jnp.zeros_like(delta_in)
    delta2 = jnp.concatenate(
        [jnp.concatenate([delta_in, zero_d], axis=1), jnp.concatenate([zero_d, delta_in], axis=1)], axis=0
    )

    for it in range(INNER):
        last = it == INNER - 1
        for j in range(4):
            coup_less = talls[j] - dcs[j] if it == 0 else talls[j]
            rhs = baux[j] + (aux_p[it, j] - dss[j]) + coup_less
            evo = mm(rhs, x2[j])
            tall = evo + dcs[j]
            evos[j] = evo
            talls[j] = tall
            g, h = pack2(mm_tn(tall, tall))
            gsend[it, j] = g
            gsend[it, j + 4] = h
        for d in range(1, 8):
            peer = lax.rem(chan + d, 8)
            send(gsend.at[it, peer], grecv.at[it, chan], g1_s.at[it, d - 1], g1_r.at[it, chan], (cuts, peer))
        if not last:
            for j in range(4):
                at_s[it, j] = (evos[j] + dss[j]) * a_rows[j : j + 1]
            halo_send(at_s.at[it], hal_t.at[it], ht_s.at[it], ht_r.at[it])
        else:
            for j in range(4):
                evo = evos[j]
                evo_o[j] = evo[:, 0:64]
                evo_o[j + 4] = evo[:, 64:128]
        grecv[it, chan] = gsend[it, chan]
        for d in range(1, 8):
            peer = lax.rem(chan + d, 8)
            arrived(grecv.at[it, peer], g1_s.at[it, 0], g1_r.at[it, peer])
        own = grecv[it, 0]
        for c in range(1, 8):
            own = own + grecv[it, c]
        gall[it, chan] = own
        for d in range(1, 8):
            peer = lax.rem(chan + d, 8)
            send(gall.at[it, chan], gall.at[it, chan], g2_s.at[it, d - 1], g2_r.at[it, chan], (cuts, peer))
        delta2t = delta2.T
        for d in range(1, 8):
            peer = lax.rem(chan + d, 8)
            arrived(gall.at[it, peer], g2_s.at[it, 0], g2_r.at[it, peer])

        scales = []
        for j in range(4):
            lefts = mm(delta2, unpack2(gall[it, j], gall[it, j + 4]))
            left_s[j] = lefts
            normal = mm(lefts, delta2t)
            trace = half_sums(jnp.sum(jnp.where(eye_b, normal, 0.0), axis=0, keepdims=True)) + EPS_TRACE
            scales.append(1.0 / jnp.sqrt(trace))
            cur = normal / trace
            bracket = 1.5 * eye - 0.5 * cur
            cr[j, :, 0:128] = mm(bracket, cur)
            cr[j, :, 128:256] = bracket

        def polar(step, carry):
            for j in range(4):
                both = cr[j]
                bracket = 1.5 * eye - 0.5 * mm(both[:, 128:256], both[:, 0:128])
                cr[j] = mm(bracket, both)
            return carry

        lax.fori_loop(0, POLAR - 2, polar, 0)
        part = jnp.zeros((128, 128), F32)
        for j in range(4):
            both = cr[j]
            root = both[:, 128:256]
            bracket = 1.5 * eye - 0.5 * mm(root, both[:, 0:128])
            root = mm(bracket, root)
            cr[j, :, 128:256] = root
            part = part + mm(root, left_s[j]) * scales[j]
        g, h = pack2(part)
        packed = g + h
        for q in range(4):
            qsend[it, q] = packed[8 * q : 8 * q + 8]
        for d in range(1, 4):
            to = lax.rem(quad + d, 4)
            send(qsend.at[it, to], qrecv.at[it, quad], q1_s.at[it, d - 1], q1_r.at[it, quad], quad_dev(to))
        qrecv[it, quad] = qsend[it, quad]
        for j in range(4):
            k2_s[j] = mm(delta2t, cr[j, :, 128:256]) * scales[j]
        for d in range(1, 4):
            frm = lax.rem(quad + d, 4)
            arrived(qrecv.at[it, frm], q1_s.at[it, 0], q1_r.at[it, frm])
        zbuf[it, zz] = (qrecv[it, 0] + qrecv[it, 1]) + (qrecv[it, 2] + qrecv[it, 3])
        for d in range(1, 8):
            to = lax.rem(zz + d, 8)
            send(zbuf.at[it, zz], zbuf.at[it, zz], z_s.at[it, d - 1], z_r.at[it, zz], z_dev(to))

        if not last:
            for n in range(2):
                arrived(hal_a.at[it, n], ha_s.at[it, n], ha_r.at[it, n])
                arrived(hal_t.at[it, n], ht_s.at[it, n], ht_r.at[it, n])
                if it == 0:
                    arrived(hal_b.at[n], hb_s.at[n], hb_r.at[n])
            vals, tars, bs = [], [], []
            for p in range(4):
                vals.append(jnp.where(low, swap(hal_a[it, 0, p]), aux_p[it, p]))
                tars.append(jnp.where(low, swap(hal_t[it, 0, p]), at_s[it, p]))
                bs.append(jnp.where(low, swap(hal_b[0, p : p + 1]), bsend[p : p + 1]))
            for p in range(4):
                vals.append(jnp.where(low, aux_p[it, p], swap(hal_a[it, 1, p])))
                tars.append(jnp.where(low, at_s[it, p], swap(hal_t[it, 1, p])))
                bs.append(jnp.where(low, bsend[p : p + 1], swap(hal_b[1, p : p + 1])))
            for sweep in range(4):
                fresh = []
                for p in range(8):
                    before = vals[p - 1] if p > 0 else swap(vals[7])
                    after = vals[p + 1] if p < 7 else swap(vals[0])
                    fresh.append(tars[p] + bs[p] * (before + after))
                vals = fresh
            for j in range(4):
                aux = jnp.where(low, vals[4 + j], vals[j])
                aux_p[it + 1, j] = aux
                dss[j] = dss[j] + evos[j] - aux
            if it + 1 < INNER - 1:
                halo_send(aux_p.at[it + 1], hal_a.at[it + 1], ha_s.at[it + 1], ha_r.at[it + 1])

        for d in range(1, 8):
            frm = lax.rem(zz + d, 8)
            arrived(zbuf.at[it, frm], z_s.at[it, 0], z_r.at[it, frm])
        total = zbuf[it, 0]
        for z in range(1, 8):
            total = total + zbuf[it, z]
        qall[it, quad] = total * (1.0 / 256.0)
        for d in range(1, 4):
            to = lax.rem(quad + d, 4)
            send(qall.at[it, quad], qall.at[it, quad], q2_s.at[it, d - 1], q2_r.at[it, quad], quad_dev(to))
        for d in range(1, 4):
            frm = lax.rem(quad + d, 4)
            arrived(qall.at[it, frm], q2_s.at[it, 0], q2_r.at[it, frm])
        packed = jnp.concatenate([qall[it, q] for q in range(4)], axis=0)
        delta2 = unpack2(packed, packed)

        for j in range(4):
            mixer = mm(k2_s[j], delta2)
            tall = talls[j]
            coup = mm(tall, mixer)
            if last:
                coup_o[j] = coup[:, 0:64]
                coup_o[j + 4] = coup[:, 64:128]
            else:
                dual = tall - coup
                dcs[j] = dual
                talls[j] = coup - dual
        if last:
            delta_o[...] = delta2[0:64, 0:64]

    for copy in sent:
        copy.wait_send()


def body(data, order, chan_factor, slice_weights, smooth_aux, coupled, smooth_dual, coupling_dual, delta):
    vm = pltpu.VMEM
    dma = pltpu.SemaphoreType.DMA
    rows = (4, 48, 128)
    anyspace = pl.BlockSpec(memory_space=pl.ANY)
    vspace = pl.BlockSpec(memory_space=pltpu.VMEM)
    return pl.pallas_call(
        kernel,
        out_shape=(
            jax.ShapeDtypeStruct((8, 48, 64), F32),
            jax.ShapeDtypeStruct((8, 48, 64), F32),
            jax.ShapeDtypeStruct((64, 64), F32),
        ),
        in_specs=[pl.BlockSpec(memory_space=pltpu.SMEM)] + [anyspace] * 8,
        out_specs=(vspace, vspace, vspace),
        scratch_shapes=[
            vm((8, 384, 128), jnp.bfloat16), vm((128, 64), jnp.bfloat16), vm((8, 64), F32),
            vm((8, 48, 64), F32), vm((8, 48, 64), F32), vm((8, 48, 64), F32), vm((8, 48, 64), F32), vm((64, 64), F32),
            vm((4, 2) + rows, F32), vm((4, 2) + rows, F32), vm(rows, F32), vm(rows, F32),
            vm((8, 32, 128), F32), vm((4, 128, 128), F32), vm((4, 128, 256), F32),
            vm((4, 128, 128), F32), vm((4, 128, 128), F32),
            vm((3, 8, 32, 128), F32), vm((3, 8, 32, 128), F32), vm((3, 8, 32, 128), F32),
            vm((3, 4, 8, 128), F32), vm((3, 4, 8, 128), F32), vm((3, 8, 8, 128), F32), vm((3, 4, 8, 128), F32),
            vm((3,) + rows, F32), vm(rows, F32), vm(rows, F32), vm(rows, F32), vm(rows, F32),
            vm((2,) + rows, F32), vm(rows, F32),
            vm((2, 2) + rows, F32), vm((2, 2) + rows, F32), vm((8, 128), F32), vm((2, 8, 128), F32),
            dma((8,)), dma((3,)), dma((4,)), dma, dma, dma((7,)), dma((8,)),
            dma((3, 7)), dma((3, 8)), dma((3, 7)), dma((3, 8)), dma((3, 3)), dma((3, 4)),
            dma((3, 7)), dma((3, 8)), dma((3, 3)), dma((3, 4)),
            dma((2, 2)), dma((2, 2)), dma((2, 2)), dma((2, 2)), dma((2,)), dma((2,)),
        ],
        compiler_params=pltpu.CompilerParams(
            collective_id=0, has_side_effects=True, vmem_limit_bytes=60 * 1024 * 1024
        ),
    )(order, data, chan_factor, slice_weights, smooth_aux, coupled, smooth_dual, coupling_dual, delta)


def solution(mesh):
    return jax.shard_map(
        body,
        mesh=mesh,
        in_specs=(
            P("cuts", None, "chan"),
            P("cuts"),
            P("chan", None),
            P("cuts", None),
            P("cuts", "chan", None),
            P("cuts", "chan", None),
            P("cuts", "chan", None),
            P("cuts", "chan", None),
            P(),
        ),
        out_specs=(P("cuts", "chan", None), P("cuts", "chan", None), P()),
        check_vma=False,
    )
```

```python
import jax
import jax.numpy as jnp
from jax import lax
from jax.experimental import pallas as pl
from jax.experimental.pallas import tpu as pltpu
from jax.sharding import PartitionSpec as P

INNER = 3
POLAR = 8
NEWTON = 7
EPS_TRACE = 1e-06
F32 = jnp.float32
MESH = pl.DeviceIdType.MESH
CHEB_A = 0.1328125 / 1.2578125
CHEB_B = -1.0 / (512.0 * 1.2578125)


BF16 = jnp.bfloat16


def split(a):
    high = a.astype(BF16)
    return high, (a - high.astype(F32)).astype(BF16)


def lhs3(a):
    high, rest = split(a)
    return jnp.concatenate([high, rest, high], axis=1)


def dot(a, b):
    return jnp.dot(a, b, preferred_element_type=F32)


def gram_of(a, b):
    left, right = [], []
    for p, q in zip(a, b):
        ph, pl_ = split(p)
        qh, ql = split(q)
        left += [ph, pl_, ph]
        right += [qh, qh, ql]
    return lax.dot_general(
        jnp.concatenate(left, axis=0), jnp.concatenate(right, axis=0), (((0,), (0,)), ((), ())),
        preferred_element_type=F32,
    )


def kernel(
    order, data_h, fac_h, w_h, aux_h, coup_h, ds_h, dc_h, delta_h,
    evo_o, coup_o, delta_o,
    data_v, fac_v, w_v, aux_v, coup_v, ds_v, dc_v, delta_v,
    psend, precv, ysend, yrecv, fg, x_s, sys_s, x_rhs, cr, left_s, k_s,
    gsend, grecv, gall, ssend, srecv, sall, qsend, qrecv, zbuf, qall,
    aux_p, dss, talls, evos, us, at_s, baux, hal_a, hal_t, bsend, hal_b,
    load_sem, px_s, px_r, py_s, py_r, fg_s, fg_r,
    g1_s, g1_r, g2_s, g2_r, s1_s, s1_r, s2_s, s2_r, q1_s, q1_r, z_s, z_r, q2_s, q2_r, ha_s, ha_r, ht_s, ht_r, hb_s, hb_r,
):
    cuts = lax.axis_index("cuts")
    chan = lax.axis_index("chan")
    core = lax.rem(cuts, 2)
    zz = lax.rem(cuts // 2, 8)
    ylo = cuts // 16
    quad = ylo * 2 + core
    xx = lax.rem(chan, 4)
    yhi = chan // 4
    left_id = lax.rem(cuts + 31, 32)
    right_id = lax.rem(cuts + 1, 32)

    def z_dev(z):
        return (ylo * 16 + z * 2 + core, chan)

    def quad_dev(q):
        return ((q // 2) * 16 + zz * 2 + lax.rem(q, 2), chan)

    sent = []

    def send(src, dst, ssem, rsem, dev):
        copy = pltpu.make_async_remote_copy(
            src_ref=src, dst_ref=dst, send_sem=ssem, recv_sem=rsem, device_id=dev, device_id_type=MESH
        )
        copy.start()
        sent.append(copy)

    def arrived(dst, ssem, rsem):
        pltpu.make_async_remote_copy(
            src_ref=dst, dst_ref=dst, send_sem=ssem, recv_sem=rsem, device_id=(left_id, chan), device_id_type=MESH
        ).wait_recv()

    loads = []
    for n, (src, dst) in enumerate(
        (
            (fac_h, fac_v), (data_h, data_v), (w_h, w_v), (aux_h, aux_v), (coup_h, coup_v),
            (ds_h, ds_v), (dc_h, dc_v), (delta_h, delta_v),
        )
    ):
        copy = pltpu.make_async_copy(src, dst, load_sem.at[n])
        copy.start()
        loads.append(copy)

    barrier = pltpu.get_barrier_semaphore()
    greet = [(cuts, lax.rem(chan + d, 8)) for d in range(1, 8)]
    greet += [z_dev(lax.rem(zz + d, 8)) for d in range(1, 8)]
    greet += [quad_dev(lax.rem(quad + d, 4)) for d in range(1, 4)]
    greet += [(left_id, chan), (right_id, chan)]
    for dev in greet:
        pl.semaphore_signal(barrier, inc=1, device_id=dev, device_id_type=MESH)

    lane = lax.broadcasted_iota(jnp.int32, (1, 128), 1)
    low = lane < 64
    high = lane >= 64
    row_i = lax.broadcasted_iota(jnp.int32, (64, 128), 0)
    col_i = lax.broadcasted_iota(jnp.int32, (64, 128), 1)
    eye_b = row_i == lax.rem(col_i, 64)
    eye = eye_b.astype(F32)
    low16 = low.astype(F32).astype(BF16)
    high16 = high.astype(F32).astype(BF16)

    def swap(v):
        return pltpu.roll(v, 64, 1)

    def widen(v):
        return jnp.concatenate([v * low16, v * high16], axis=0)

    def rhs3(a):
        first, rest = split(a)
        first, rest = widen(first), widen(rest)
        return jnp.concatenate([first, first, rest], axis=0)

    def mm(a, b):
        return dot(lhs3(a), rhs3(b))

    def narrow(t):
        return jnp.where(low, t[0:64], t[64:128])

    def unpack(p):
        q = swap(p)
        return jnp.concatenate([jnp.where(low, p, q), jnp.where(low, q, p)], axis=0)

    def transposed(c):
        return jnp.concatenate([c, c], axis=0).T[0:64]

    def half_sums(v):
        zero = jnp.zeros_like(v)
        lo = jnp.sum(jnp.where(low, v, zero), axis=1, keepdims=True)
        hi = jnp.sum(jnp.where(low, zero, v), axis=1, keepdims=True)
        return jnp.where(low, lo, hi)

    loads[0].wait()
    fac = fac_v[...]
    partial_gram = lax.dot_general(fac, fac, (((0,), (0,)), ((), ())), preferred_element_type=F32)
    fg[chan] = jnp.concatenate([partial_gram[0:32], partial_gram[32:64]], axis=1)
    pl.semaphore_wait(barrier, len(greet))
    for d in range(1, 8):
        peer = lax.rem(chan + d, 8)
        send(fg.at[chan], fg.at[chan], fg_s.at[d - 1], fg_r.at[chan], (cuts, peer))

    zero_fac = jnp.zeros_like(fac)
    fac2 = jnp.concatenate(
        [jnp.concatenate([fac, zero_fac], axis=1), jnp.concatenate([zero_fac, fac], axis=1)], axis=0
    )
    loads[1].wait()
    for j in range(4):
        first = data_v[lax.rem(order[j], 8)]
        second = data_v[lax.rem(order[j + 4], 8)]
        out = jnp.dot(jnp.concatenate([first, second], axis=1), fac2, preferred_element_type=F32)
        for c in range(8):
            psend[c % 4, c // 4, j] = out[48 * c : 48 * c + 48]
    for d in (2, 1, 3):
        to = lax.rem(xx + d, 4)
        send(psend.at[to], precv.at[xx], px_s.at[d - 1], px_r.at[xx], (cuts, yhi * 4 + to))

    for n in range(2, 8):
        loads[n].wait()
    for j in range(4):
        aux_p[0, j] = jnp.concatenate([aux_v[j], aux_v[j + 4]], axis=1)
        dss[j] = jnp.concatenate([ds_v[j], ds_v[j + 4]], axis=1)
        dual = jnp.concatenate([dc_v[j], dc_v[j + 4]], axis=1)
        talls[j] = dual
        us[j] = jnp.concatenate([coup_v[j], coup_v[j + 4]], axis=1) - dual

    def halo_send(src, dst, ssem, rsem):
        send(src, dst.at[0], ssem.at[0], rsem.at[0], (right_id, chan))
        send(src, dst.at[1], ssem.at[1], rsem.at[1], (left_id, chan))

    halo_send(aux_p.at[0], hal_a.at[0], ha_s.at[0], ha_r.at[0])

    for d in range(1, 8):
        peer = lax.rem(chan + d, 8)
        arrived(fg.at[peer], fg_s.at[0], fg_r.at[peer])
    gram_sum = fg[0]
    for c in range(1, 8):
        gram_sum = gram_sum + fg[c]
    gram2 = unpack(gram_sum)
    w = w_v[...]
    w2 = jnp.concatenate([w[0:4], w[4:8]], axis=1)
    diag_row = jnp.sum(jnp.where(eye_b, gram2, 0.0), axis=0, keepdims=True)
    rho = half_sums(w2 * w2 * diag_row) * (1.0 / 64.0)
    w_over = w2 / rho
    b_rows = 2.0 / (rho + 4.0)
    a_rows = rho / (rho + 4.0)
    bsend[0:4] = b_rows
    bsend[4:8] = b_rows
    halo_send(bsend, hal_b, hb_s, hb_r)
    for j in range(4):
        w_col = half_sums(jnp.where(eye_b, w2[j : j + 1], 0.0))
        system = gram2 * w_col * w_over[j : j + 1] + 2.0 * eye
        sys_s[j] = lhs3(system)
        x_s[j] = CHEB_A * eye + CHEB_B * system

    def newton(step, carry):
        for j in range(4):
            x = x_s[j]
            x_s[j] = mm(x, 2.0 * eye - dot(sys_s[j], rhs3(x)))
        return carry

    lax.fori_loop(0, NEWTON, newton, 0)
    for j in range(4):
        x_rhs[j] = rhs3(x_s[j])

    for d in range(1, 4):
        frm = lax.rem(xx + d, 4)
        arrived(precv.at[frm], px_s.at[0], px_r.at[frm])
    for j in range(4):
        total = psend[xx, 1 - yhi, j]
        for d in range(1, 4):
            total = total + precv[lax.rem(xx + d, 4), 1 - yhi, j]
        ysend[j] = total
    send(ysend, yrecv, py_s, py_r, (cuts, (1 - yhi) * 4 + xx))
    for j in range(4):
        total = psend[xx, yhi, j]
        for d in range(1, 4):
            total = total + precv[lax.rem(xx + d, 4), yhi, j]
        baux[j] = total
    arrived(yrecv, py_s, py_r)
    for j in range(4):
        baux[j] = (baux[j] + yrecv[j]) * w_over[j : j + 1]

    delta_in = delta_v[...]
    delta = jnp.concatenate([delta_in, delta_in], axis=1)

    def spread(buf, ssem, rsem, own):
        buf[chan] = own
        for d in range(1, 8):
            peer = lax.rem(chan + d, 8)
            send(buf.at[chan], buf.at[chan], ssem.at[d - 1], rsem.at[chan], (cuts, peer))

    def from_chan(buf, ssem, rsem):
        for d in range(1, 8):
            peer = lax.rem(chan + d, 8)
            arrived(buf.at[peer], ssem.at[0], rsem.at[peer])

    def scatter(src, dst, ssem, rsem):
        for d in range(1, 8):
            peer = lax.rem(chan + d, 8)
            send(src.at[peer], dst.at[chan], ssem.at[d - 1], rsem.at[chan], (cuts, peer))
        dst[chan] = src[chan]

    def total_of(buf):
        total = buf[0]
        for c in range(1, 8):
            total = total + buf[c]
        return total

    def smooth(it):
        for n in range(2):
            arrived(hal_a.at[it, n], ha_s.at[it, n], ha_r.at[it, n])
            arrived(hal_t.at[it, n], ht_s.at[it, n], ht_r.at[it, n])
            if it == 0:
                arrived(hal_b.at[n], hb_s.at[n], hb_r.at[n])
        vals, tars, bs = [], [], []
        for p in range(4):
            vals.append(jnp.where(low, swap(hal_a[it, 0, p]), aux_p[it, p]))
            tars.append(jnp.where(low, swap(hal_t[it, 0, p]), at_s[it, p]))
            bs.append(jnp.where(low, swap(hal_b[0, p : p + 1]), bsend[p : p + 1]))
        for p in range(4):
            vals.append(jnp.where(low, aux_p[it, p], swap(hal_a[it, 1, p])))
            tars.append(jnp.where(low, at_s[it, p], swap(hal_t[it, 1, p])))
            bs.append(jnp.where(low, bsend[p : p + 1], swap(hal_b[1, p : p + 1])))
        for sweep in range(4):
            fresh = []
            for p in range(8):
                before = vals[p - 1] if p > 0 else swap(vals[7])
                after = vals[p + 1] if p < 7 else swap(vals[0])
                fresh.append(tars[p] + bs[p] * (before + after))
            vals = fresh
        for j in range(4):
            aux = jnp.where(low, vals[4 + j], vals[j])
            dual = dss[j] + evos[j] - aux
            if it == 0:
                aux_p[1, j] = aux
            dss[j] = dual
            us[j] = dot(lhs3(baux[j] + (aux - dual)), x_rhs[j])
        if it == 0:
            halo_send(aux_p.at[1], hal_a.at[1], ha_s.at[1], ha_r.at[1])
        for j in range(4):
            u, tall = us[j], talls[j]
            guu = narrow(gram_of([u], [u]))
            gtu = narrow(gram_of([tall], [u]))
            for h in range(2):
                ssend[it, 2 * j + h, 0] = guu[32 * h : 32 * h + 32]
                ssend[it, 2 * j + h, 1] = gtu[32 * h : 32 * h + 32]
        scatter(ssend.at[it], srecv.at[it], s1_s.at[it], s1_r.at[it])

    def gather_sums(it):
        from_chan(srecv.at[it], s1_s.at[it], s1_r.at[it])
        spread(sall.at[it], s2_s.at[it], s2_r.at[it], total_of(srecv.at[it]))

    def polar(step, carry):
        for j in range(4):
            both = cr[j]
            root = both[:, 128:256]
            ch, cl = split(both[:, 0:128])
            rh, rl = split(root)
            ch, cl = widen(ch), widen(cl)
            prod = dot(lhs3(root), jnp.concatenate([ch, ch, cl], axis=0))
            firsts = jnp.concatenate([ch, widen(rh)], axis=1)
            rests = jnp.concatenate([cl, widen(rl)], axis=1)
            bracket = 1.5 * eye - 0.5 * prod
            cr[j] = dot(lhs3(bracket), jnp.concatenate([firsts, firsts, rests], axis=0))
        return carry

    for j in range(4):
        dual = talls[j]
        evo = dot(lhs3(baux[j] + (aux_p[0, j] - dss[j]) + us[j]), x_rhs[j])
        tall = evo + dual
        evos[j] = evo
        talls[j] = tall
        part = narrow(gram_of([tall], [tall]))
        gsend[2 * j] = part[0:32]
        gsend[2 * j + 1] = part[32:64]
    scatter(gsend, grecv, g1_s, g1_r)
    for j in range(4):
        at_s[0, j] = (evos[j] + dss[j]) * a_rows[j : j + 1]
    halo_send(at_s.at[0], hal_t.at[0], ht_s.at[0], ht_r.at[0])
    from_chan(grecv, g1_s, g1_r)
    spread(gall, g2_s, g2_r, total_of(grecv))
    smooth(0)
    from_chan(gall, g2_s, g2_r)
    grams = [jnp.concatenate([gall[2 * j], gall[2 * j + 1]], axis=0) for j in range(4)]

    for it in range(INNER):
        last = it == INNER - 1
        delta_t = transposed(delta)
        delta_l = lhs3(delta)
        delta_r = rhs3(delta_t)
        scales = []
        for j in range(4):
            lefts = dot(delta_l, rhs3(grams[j]))
            left_s[j] = lefts
            normal = dot(lhs3(lefts), delta_r)
            trace = half_sums(jnp.sum(jnp.where(eye_b, normal, 0.0), axis=0, keepdims=True)) + EPS_TRACE
            scales.append(1.0 / jnp.sqrt(trace))
            cur = normal / trace
            bracket = 1.5 * eye - 0.5 * cur
            cr[j, :, 0:128] = mm(bracket, cur)
            cr[j, :, 128:256] = bracket

        if it == 0:
            lax.fori_loop(0, 3, polar, 0)
            gather_sums(0)
            lax.fori_loop(0, POLAR - 5, polar, 0)
        elif it == 1:
            lax.fori_loop(0, 2, polar, 0)
            smooth(1)
            lax.fori_loop(0, POLAR - 4, polar, 0)
        else:
            lax.fori_loop(0, POLAR - 2, polar, 0)
        part = jnp.zeros((64, 128), F32)
        for j in range(4):
            both = cr[j]
            root = both[:, 128:256]
            root = mm(1.5 * eye - 0.5 * mm(root, both[:, 0:128]), root)
            cr[j, :, 128:256] = root
            part = part + mm(root, left_s[j]) * scales[j]
        part = part + swap(part)
        packed = jnp.where(low, part[0:32], part[32:64])
        for q in range(4):
            qsend[it, q] = packed[8 * q : 8 * q + 8]
        for d in range(1, 4):
            to = lax.rem(quad + d, 4)
            send(qsend.at[it, to], qrecv.at[it, quad], q1_s.at[it, d - 1], q1_r.at[it, quad], quad_dev(to))
        qrecv[it, quad] = qsend[it, quad]
        if it == 1:
            gather_sums(1)
        delta_tl = lhs3(delta_t)
        for j in range(4):
            k_s[j] = dot(delta_tl, rhs3(cr[j, :, 128:256])) * scales[j]
        for d in range(1, 4):
            frm = lax.rem(quad + d, 4)
            arrived(qrecv.at[it, frm], q1_s.at[it, 0], q1_r.at[it, frm])
        zbuf[it, zz] = (qrecv[it, 0] + qrecv[it, 1]) + (qrecv[it, 2] + qrecv[it, 3])
        for d in range(1, 8):
            to = lax.rem(zz + d, 8)
            send(zbuf.at[it, zz], zbuf.at[it, zz], z_s.at[it, d - 1], z_r.at[it, zz], z_dev(to))
        for d in range(1, 8):
            frm = lax.rem(zz + d, 8)
            arrived(zbuf.at[it, frm], z_s.at[it, 0], z_r.at[it, frm])
        qall[it, quad] = total_of(zbuf.at[it]) * (1.0 / 256.0)
        for d in range(1, 4):
            to = lax.rem(quad + d, 4)
            send(qall.at[it, quad], qall.at[it, quad], q2_s.at[it, d - 1], q2_r.at[it, quad], quad_dev(to))
        if not last:
            from_chan(sall.at[it], s2_s.at[it], s2_r.at[it])
        for d in range(1, 4):
            frm = lax.rem(quad + d, 4)
            arrived(qall.at[it, frm], q2_s.at[it, 0], q2_r.at[it, frm])
        delta = unpack(jnp.concatenate([qall[it, q] for q in range(4)], axis=0))
        fresh_r = rhs3(delta)

        if last:
            for j in range(4):
                mixer = dot(lhs3(k_s[j]), fresh_r)
                coup = mm(talls[j], mixer)
                coup_o[j] = coup[:, 0:64]
                coup_o[j + 4] = coup[:, 64:128]
            delta_o[...] = delta[:, 0:64]
        else:
            fresh = []
            for j in range(4):
                mixer = dot(lhs3(k_s[j]), fresh_r)
                turn = dot(lhs3(2.0 * mixer - eye), x_rhs[j])
                tall = talls[j]
                both = dot(lhs3(tall), jnp.concatenate([rhs3(turn), rhs3(mixer)], axis=1))
                evo = us[j] + both[:, 0:128]
                evos[j] = evo
                talls[j] = evo + (tall - both[:, 128:256])
                if it == 0:
                    at_s[1, j] = (evo + dss[j]) * a_rows[j : j + 1]
                else:
                    evo_o[j] = evo[:, 0:64]
                    evo_o[j + 4] = evo[:, 64:128]
                step = turn + (eye - mixer)
                guu = jnp.concatenate([sall[it, 2 * j, 0], sall[it, 2 * j + 1, 0]], axis=0)
                gtu = jnp.concatenate([sall[it, 2 * j, 1], sall[it, 2 * j + 1, 1]], axis=0)
                side = gtu + 0.5 * mm(grams[j], step)
                fresh.append(guu + narrow(gram_of([step, side], [side, step])))
            if it == 0:
                halo_send(at_s.at[1], hal_t.at[1], ht_s.at[1], ht_r.at[1])
            grams = fresh

    for copy in sent:
        copy.wait_send()


def body(data, order, chan_factor, slice_weights, smooth_aux, coupled, smooth_dual, coupling_dual, delta):
    vm = pltpu.VMEM
    dma = pltpu.SemaphoreType.DMA
    rows = (4, 48, 128)
    anyspace = pl.BlockSpec(memory_space=pl.ANY)
    vspace = pl.BlockSpec(memory_space=pltpu.VMEM)
    return pl.pallas_call(
        kernel,
        out_shape=(
            jax.ShapeDtypeStruct((8, 48, 64), F32),
            jax.ShapeDtypeStruct((8, 48, 64), F32),
            jax.ShapeDtypeStruct((64, 64), F32),
        ),
        in_specs=[pl.BlockSpec(memory_space=pltpu.SMEM)] + [anyspace] * 8,
        out_specs=(vspace, vspace, vspace),
        scratch_shapes=[
            vm((8, 384, 128), jnp.bfloat16), vm((128, 64), jnp.bfloat16), vm((8, 64), F32),
            vm((8, 48, 64), F32), vm((8, 48, 64), F32), vm((8, 48, 64), F32), vm((8, 48, 64), F32), vm((64, 64), F32),
            vm((4, 2) + rows, F32), vm((4, 2) + rows, F32), vm(rows, F32), vm(rows, F32),
            vm((8, 32, 128), F32), vm((4, 64, 128), F32), vm((4, 64, 384), BF16), vm((4, 384, 128), BF16),
            vm((4, 64, 256), F32), vm((4, 64, 128), F32), vm((4, 64, 128), F32),
            vm((8, 32, 128), F32), vm((8, 32, 128), F32), vm((8, 32, 128), F32),
            vm((2, 8, 2, 32, 128), F32), vm((2, 8, 2, 32, 128), F32), vm((2, 8, 2, 32, 128), F32),
            vm((3, 4, 8, 128), F32), vm((3, 4, 8, 128), F32), vm((3, 8, 8, 128), F32), vm((3, 4, 8, 128), F32),
            vm((2,) + rows, F32), vm(rows, F32), vm(rows, F32), vm(rows, F32), vm(rows, F32),
            vm((2,) + rows, F32), vm(rows, F32),
            vm((2, 2) + rows, F32), vm((2, 2) + rows, F32), vm((8, 128), F32), vm((2, 8, 128), F32),
            dma((8,)), dma((3,)), dma((4,)), dma, dma, dma((7,)), dma((8,)),
            dma((7,)), dma((8,)), dma((7,)), dma((8,)),
            dma((2, 7)), dma((2, 8)), dma((2, 7)), dma((2, 8)),
            dma((3, 3)), dma((3, 4)), dma((3, 7)), dma((3, 8)), dma((3, 3)), dma((3, 4)),
            dma((2, 2)), dma((2, 2)), dma((2, 2)), dma((2, 2)), dma((2,)), dma((2,)),
        ],
        compiler_params=pltpu.CompilerParams(
            collective_id=0, has_side_effects=True, vmem_limit_bytes=60 * 1024 * 1024
        ),
    )(order, data, chan_factor, slice_weights, smooth_aux, coupled, smooth_dual, coupling_dual, delta)


def solution(mesh):
    return jax.shard_map(
        body,
        mesh=mesh,
        in_specs=(
            P("cuts", None, "chan"),
            P("cuts"),
            P("chan", None),
            P("cuts", None),
            P("cuts", "chan", None),
            P("cuts", "chan", None),
            P("cuts", "chan", None),
            P("cuts", "chan", None),
            P(),
        ),
        out_specs=(P("cuts", "chan", None), P("cuts", "chan", None), P()),
        check_vma=False,
    )
```

```python
import jax
import jax.numpy as jnp
from jax import lax
from jax.experimental import pallas as pl
from jax.experimental.pallas import tpu as pltpu
from jax.sharding import PartitionSpec as P

INNER = 3
POLAR = 8
NEWTON = 7
EPS_TRACE = 1e-06
F32 = jnp.float32
MESH = pl.DeviceIdType.MESH
CHEB_A = 0.1328125 / 1.2578125
CHEB_B = -1.0 / (512.0 * 1.2578125)


BF16 = jnp.bfloat16


def split(a):
    high = a.astype(BF16)
    return high, (a - high.astype(F32)).astype(BF16)


def lhs3(a):
    high, rest = split(a)
    return jnp.concatenate([high, rest, high], axis=1)


def dot(a, b):
    return jnp.dot(a, b, preferred_element_type=F32)


def gram_of(a, b):
    left, right = [], []
    for p, q in zip(a, b):
        ph, pl_ = split(p)
        qh, ql = split(q)
        left += [ph, pl_, ph]
        right += [qh, qh, ql]
    return lax.dot_general(
        jnp.concatenate(left, axis=0), jnp.concatenate(right, axis=0), (((0,), (0,)), ((), ())),
        preferred_element_type=F32,
    )


def kernel(
    order, data_h, fac_h, w_h, aux_h, coup_h, ds_h, dc_h, delta_h,
    evo_o, coup_o, delta_o,
    data_v, fac_v, w_v, rows_v, delta_v,
    psend, precv, ysend, yrecv, fg, x_s, sys_s, x_rhs, cr, left_s, k_s,
    gsend, grecv, gall, ssend, srecv, sall, qsend, qrecv, zbuf, qall,
    aux_p, dss, talls, evos, us, mix_s, at_s, baux, hal_a, hal_t, bsend, hal_b,
    load_sem, px_s, px_r, py_s, py_r, fg_s, fg_r, g1_s, g1_r, g2_s, g2_r, s1_s, s1_r, s2_s, s2_r,
    q1_s, q1_r, z_s, z_r, q2_s, q2_r, ha_s, ha_r, ht_s, ht_r, hb_s, hb_r,
):
    cuts = lax.axis_index("cuts")
    chan = lax.axis_index("chan")
    core = lax.rem(cuts, 2)
    zz = lax.rem(cuts // 2, 8)
    ylo = cuts // 16
    quad = ylo * 2 + core
    xx = lax.rem(chan, 4)
    yhi = chan // 4
    left_id = lax.rem(cuts + 31, 32)
    right_id = lax.rem(cuts + 1, 32)

    def z_dev(z):
        return (ylo * 16 + z * 2 + core, chan)

    def quad_dev(q):
        return ((q // 2) * 16 + zz * 2 + lax.rem(q, 2), chan)

    def send(src, dst, ssem, rsem, dev):
        pltpu.make_async_remote_copy(
            src_ref=src, dst_ref=dst, send_sem=ssem, recv_sem=rsem, device_id=dev, device_id_type=MESH
        ).start()

    def whole(ref, ssem, rsem):
        return pltpu.make_async_remote_copy(
            src_ref=ref, dst_ref=ref, send_sem=ssem, recv_sem=rsem, device_id=(left_id, chan), device_id_type=MESH
        )

    def arrived(ref, ssem, rsem):
        whole(ref, ssem, rsem).wait_recv()

    def load(src, dst, n):
        return pltpu.make_async_copy(src, dst, load_sem.at[n])

    load(fac_h, fac_v, 0).start()
    load(data_h, data_v, 1).start()
    load(w_h, w_v, 2).start()
    for n, src in enumerate((aux_h, coup_h, ds_h, dc_h)):
        load(src, rows_v.at[n], 3).start()
    load(delta_h, delta_v, 4).start()

    barrier = pltpu.get_barrier_semaphore()
    greet = [(cuts, lax.rem(chan + d, 8)) for d in range(1, 8)]
    greet += [z_dev(lax.rem(zz + d, 8)) for d in range(1, 8)]
    greet += [quad_dev(lax.rem(quad + d, 4)) for d in range(1, 4)]
    greet += [(left_id, chan), (right_id, chan)]
    for dev in greet:
        pl.semaphore_signal(barrier, inc=1, device_id=dev, device_id_type=MESH)

    lane = lax.broadcasted_iota(jnp.int32, (1, 128), 1)
    low = lane < 64
    high = lane >= 64
    row_i = lax.broadcasted_iota(jnp.int32, (64, 128), 0)
    col_i = lax.broadcasted_iota(jnp.int32, (64, 128), 1)
    eye_b = row_i == lax.rem(col_i, 64)
    eye = eye_b.astype(F32)
    low16 = low.astype(F32).astype(BF16)
    high16 = high.astype(F32).astype(BF16)

    def swap(v):
        return pltpu.roll(v, 64, 1)

    def widen(v):
        return jnp.concatenate([v * low16, v * high16], axis=0)

    def rhs3(a):
        first, rest = split(a)
        first, rest = widen(first), widen(rest)
        return jnp.concatenate([first, first, rest], axis=0)

    def mm(a, b):
        return dot(lhs3(a), rhs3(b))

    def narrow(t):
        return jnp.where(low, t[0:64], t[64:128])

    def unpack(p):
        q = swap(p)
        return jnp.concatenate([jnp.where(low, p, q), jnp.where(low, q, p)], axis=0)

    def transposed(c):
        return jnp.concatenate([c, c], axis=0).T[0:64]

    def half_sums(v):
        zero = jnp.zeros_like(v)
        lo = jnp.sum(jnp.where(low, v, zero), axis=1, keepdims=True)
        hi = jnp.sum(jnp.where(low, zero, v), axis=1, keepdims=True)
        return jnp.where(low, lo, hi)

    load(fac_h, fac_v, 0).wait()
    fac = fac_v[...]
    nt = (((1,), (1,)), ((), ()))
    partial_gram = lax.dot_general(fac, fac, nt, preferred_element_type=F32)
    fg[chan] = jnp.concatenate([partial_gram[0:32], partial_gram[32:64]], axis=1)
    pl.semaphore_wait(barrier, len(greet))
    for d in range(1, 8):
        peer = lax.rem(chan + d, 8)
        send(fg.at[chan], fg.at[chan], fg_s, fg_r, (cuts, peer))

    zero_fac = jnp.zeros_like(fac)
    fac2 = jnp.concatenate(
        [jnp.concatenate([fac, zero_fac], axis=1), jnp.concatenate([zero_fac, fac], axis=1)], axis=0
    )
    load(data_h, data_v, 1).wait()
    for j in range(4):
        first = data_v[lax.rem(order[j], 8)]
        second = data_v[lax.rem(order[j + 4], 8)]
        out = lax.dot_general(jnp.concatenate([first, second], axis=1), fac2, nt, preferred_element_type=F32)
        for c in range(8):
            psend[j, c % 4, c // 4] = out[48 * c : 48 * c + 48]
        for d in (2, 1, 3):
            to = lax.rem(xx + d, 4)
            send(psend.at[j, to], precv.at[j, xx], px_s, px_r.at[j], (cuts, yhi * 4 + to))

    load(w_h, w_v, 2).wait()
    load(rows_v, rows_v, 3).wait()
    load(delta_h, delta_v, 4).wait()

    def pair(n, j):
        return jnp.concatenate([rows_v[n, j], rows_v[n, j + 4]], axis=1)

    for j in range(4):
        aux_p[0, j] = pair(0, j)
        dss[j] = pair(2, j)
        dual = pair(3, j)
        talls[j] = dual
        us[j] = pair(1, j) - dual

    def halo_send(src, dst, ssem, rsem):
        send(src, dst.at[0], ssem, rsem, (right_id, chan))
        send(src, dst.at[1], ssem, rsem, (left_id, chan))

    halo_send(aux_p.at[0], hal_a.at[0], ha_s, ha_r.at[0])

    arrived(fg.at[pl.ds(0, 7)], fg_s, fg_r)
    gram_sum = fg[0]
    for c in range(1, 8):
        gram_sum = gram_sum + fg[c]
    gram2 = unpack(gram_sum)
    w = w_v[...]
    w2 = jnp.concatenate([w[0:4], w[4:8]], axis=1)
    diag_row = jnp.sum(jnp.where(eye_b, gram2, 0.0), axis=0, keepdims=True)
    rho = half_sums(w2 * w2 * diag_row) * (1.0 / 64.0)
    w_over = w2 / rho
    b_rows = 2.0 / (rho + 4.0)
    a_rows = rho / (rho + 4.0)
    bsend[0:4] = b_rows
    bsend[4:8] = b_rows
    halo_send(bsend, hal_b, hb_s, hb_r)
    for j in range(4):
        w_col = half_sums(jnp.where(eye_b, w2[j : j + 1], 0.0))
        system = gram2 * w_col * w_over[j : j + 1] + 2.0 * eye
        sys_s[j] = lhs3(system)
        x_s[j] = CHEB_A * eye + CHEB_B * system

    def newton(step, carry):
        for j in range(4):
            x = x_s[j]
            x_s[j] = mm(x, 2.0 * eye - dot(sys_s[j], rhs3(x)))
        return carry

    def forward(j):
        arrived(precv.at[j, pl.ds(0, 3)], px_s, px_r.at[j])
        total = psend[j, xx, 1 - yhi]
        for d in range(1, 4):
            total = total + precv[j, lax.rem(xx + d, 4), 1 - yhi]
        ysend[j] = total
        send(ysend.at[j], yrecv.at[j], py_s, py_r.at[j], (cuts, (1 - yhi) * 4 + xx))
        total = psend[j, xx, yhi]
        for d in range(1, 4):
            total = total + precv[j, lax.rem(xx + d, 4), yhi]
        baux[j] = total

    lax.fori_loop(0, 2, newton, 0)
    forward(0)
    lax.fori_loop(0, 3, newton, 0)
    forward(1)
    lax.fori_loop(0, NEWTON - 5, newton, 0)
    forward(2)
    for j in range(4):
        x_rhs[j] = rhs3(x_s[j])
    forward(3)

    delta_in = delta_v[...]
    delta = jnp.concatenate([delta_in, delta_in], axis=1)

    def spread(buf, ssem, rsem, own):
        buf[chan] = own
        for d in range(1, 8):
            send(buf.at[chan], buf.at[chan], ssem, rsem, (cuts, lax.rem(chan + d, 8)))

    def scatter(src, dst, ssem, rsem):
        for d in range(1, 8):
            peer = lax.rem(chan + d, 8)
            send(src.at[peer], dst.at[chan], ssem, rsem, (cuts, peer))
        dst[chan] = src[chan]

    def from_chan(buf, ssem, rsem):
        arrived(buf.at[pl.ds(0, 7)], ssem, rsem)

    def total_of(buf):
        total = buf[0]
        for c in range(1, 8):
            total = total + buf[c]
        return total

    def smooth(it):
        arrived(hal_a.at[it], ha_s, ha_r.at[it])
        arrived(hal_t.at[it], ht_s, ht_r.at[it])
        if it == 0:
            arrived(hal_b, hb_s, hb_r)
        vals, tars, bs = [], [], []
        for p in range(4):
            vals.append(jnp.where(low, swap(hal_a[it, 0, p]), aux_p[it, p]))
            tars.append(jnp.where(low, swap(hal_t[it, 0, p]), at_s[it, p]))
            bs.append(jnp.where(low, swap(hal_b[0, p : p + 1]), bsend[p : p + 1]))
        for p in range(4):
            vals.append(jnp.where(low, aux_p[it, p], swap(hal_a[it, 1, p])))
            tars.append(jnp.where(low, at_s[it, p], swap(hal_t[it, 1, p])))
            bs.append(jnp.where(low, bsend[p : p + 1], swap(hal_b[1, p : p + 1])))
        for sweep in range(4):
            fresh = []
            for p in range(8):
                before = vals[p - 1] if p > 0 else swap(vals[7])
                after = vals[p + 1] if p < 7 else swap(vals[0])
                fresh.append(tars[p] + bs[p] * (before + after))
            vals = fresh
        for j in range(4):
            aux = jnp.where(low, vals[4 + j], vals[j])
            dual = dss[j] + evos[j] - aux
            if it == 0:
                aux_p[1, j] = aux
            dss[j] = dual
            us[j] = dot(lhs3(baux[j] + (aux - dual)), x_rhs[j])
        if it == 0:
            halo_send(aux_p.at[1], hal_a.at[1], ha_s, ha_r.at[1])
        for j in range(4):
            u, tall = us[j], talls[j]
            guu = narrow(gram_of([u], [u]))
            gtu = narrow(gram_of([tall], [u]))
            for h in range(2):
                ssend[it, 2 * j + h, 0] = guu[32 * h : 32 * h + 32]
                ssend[it, 2 * j + h, 1] = gtu[32 * h : 32 * h + 32]
        scatter(ssend.at[it], srecv.at[it], s1_s, s1_r.at[it])

    def gather_sums(it):
        from_chan(srecv.at[it], s1_s, s1_r.at[it])
        spread(sall.at[it], s2_s, s2_r.at[it], total_of(srecv.at[it]))

    def rows_of(j):
        tall = talls[j]
        both = dot(lhs3(tall), mix_s[j])
        evo = us[j] + both[:, 0:128]
        return evo, evo + (tall - both[:, 128:256])

    def polar(step, carry):
        for j in range(4):
            both = cr[j]
            root = both[:, 128:256]
            ch, cl = split(both[:, 0:128])
            rh, rl = split(root)
            ch, cl = widen(ch), widen(cl)
            prod = dot(lhs3(root), jnp.concatenate([ch, ch, cl], axis=0))
            firsts = jnp.concatenate([ch, widen(rh)], axis=1)
            rests = jnp.concatenate([cl, widen(rl)], axis=1)
            bracket = 1.5 * eye - 0.5 * prod
            cr[j] = dot(lhs3(bracket), jnp.concatenate([firsts, firsts, rests], axis=0))
        return carry

    for j in range(4):
        arrived(yrecv.at[j], py_s, py_r.at[j])
        baux[j] = (baux[j] + yrecv[j]) * w_over[j : j + 1]
        dual = talls[j]
        evo = dot(lhs3(baux[j] + (aux_p[0, j] - dss[j]) + us[j]), x_rhs[j])
        tall = evo + dual
        evos[j] = evo
        talls[j] = tall
        part = narrow(gram_of([tall], [tall]))
        gsend[2 * j] = part[0:32]
        gsend[2 * j + 1] = part[32:64]
    scatter(gsend, grecv, g1_s, g1_r)
    for j in range(4):
        at_s[0, j] = (evos[j] + dss[j]) * a_rows[j : j + 1]
    halo_send(at_s.at[0], hal_t.at[0], ht_s, ht_r.at[0])
    from_chan(grecv, g1_s, g1_r)
    spread(gall, g2_s, g2_r, total_of(grecv))
    smooth(0)
    from_chan(gall, g2_s, g2_r)
    grams = [jnp.concatenate([gall[2 * j], gall[2 * j + 1]], axis=0) for j in range(4)]

    for it in range(INNER):
        last = it == INNER - 1
        delta_t = transposed(delta)
        delta_l = lhs3(delta)
        delta_r = rhs3(delta_t)
        scales = []
        for j in range(4):
            lefts = dot(delta_l, rhs3(grams[j]))
            left_s[j] = lefts
            normal = dot(lhs3(lefts), delta_r)
            trace = half_sums(jnp.sum(jnp.where(eye_b, normal, 0.0), axis=0, keepdims=True)) + EPS_TRACE
            scales.append(1.0 / jnp.sqrt(trace))
            cur = normal / trace
            bracket = 1.5 * eye - 0.5 * cur
            cr[j, :, 0:128] = mm(bracket, cur)
            cr[j, :, 128:256] = bracket

        if it == 0:
            lax.fori_loop(0, 3, polar, 0)
            gather_sums(0)
            lax.fori_loop(0, POLAR - 5, polar, 0)
        elif it == 1:
            lax.fori_loop(0, 2, polar, 0)
            smooth(1)
            lax.fori_loop(0, POLAR - 4, polar, 0)
        else:
            lax.fori_loop(0, POLAR - 2, polar, 0)
        part = jnp.zeros((64, 128), F32)
        for j in range(4):
            both = cr[j]
            root = both[:, 128:256]
            root = mm(1.5 * eye - 0.5 * mm(root, both[:, 0:128]), root)
            cr[j, :, 128:256] = root
            part = part + mm(root, left_s[j]) * scales[j]
        part = part + swap(part)
        packed = jnp.where(low, part[0:32], part[32:64])
        for q in range(4):
            qsend[it * 4 + q] = packed[8 * q : 8 * q + 8]
        for d in range(1, 4):
            to = lax.rem(quad + d, 4)
            send(qsend.at[it * 4 + to], qrecv.at[it, quad], q1_s, q1_r.at[it], quad_dev(to))
        qrecv[it, quad] = qsend[it * 4 + quad]
        if it == 1:
            gather_sums(1)
        delta_tl = lhs3(delta_t)
        for j in range(4):
            k_s[j] = dot(delta_tl, rhs3(cr[j, :, 128:256])) * scales[j]
        arrived(qrecv.at[it, pl.ds(0, 3)], q1_s, q1_r.at[it])
        zbuf[it * 8 + zz] = (qrecv[it, 0] + qrecv[it, 1]) + (qrecv[it, 2] + qrecv[it, 3])
        for d in (4, 3, 5, 2, 6, 1, 7):
            slot = zbuf.at[it * 8 + zz]
            send(slot, slot, z_s, z_r.at[it], z_dev(lax.rem(zz + d, 8)))
        if last:
            for j in range(4):
                evo, tall = rows_of(j)
                talls[j] = tall
                evo_o[j] = evo[:, 0:64]
                evo_o[j + 4] = evo[:, 64:128]
        arrived(zbuf.at[pl.ds(it * 8, 7)], z_s, z_r.at[it])
        total = zbuf[it * 8]
        for z in range(1, 8):
            total = total + zbuf[it * 8 + z]
        qall[it * 4 + quad] = total * (1.0 / 256.0)
        for d in range(1, 4):
            slot = qall.at[it * 4 + quad]
            send(slot, slot, q2_s, q2_r.at[it], quad_dev(lax.rem(quad + d, 4)))
        if not last:
            from_chan(sall.at[it], s2_s, s2_r.at[it])
        arrived(qall.at[pl.ds(it * 4, 3)], q2_s, q2_r.at[it])
        delta = unpack(jnp.concatenate([qall[it * 4 + q] for q in range(4)], axis=0))
        fresh_r = rhs3(delta)

        if last:
            for j in range(4):
                mixer = dot(lhs3(k_s[j]), fresh_r)
                coup = mm(talls[j], mixer)
                coup_o[j] = coup[:, 0:64]
                coup_o[j + 4] = coup[:, 64:128]
            delta_o[...] = delta[:, 0:64]
        else:
            fresh = []
            for j in range(4):
                mixer = dot(lhs3(k_s[j]), fresh_r)
                turn = dot(lhs3(2.0 * mixer - eye), x_rhs[j])
                mix_s[j, :, 0:128] = rhs3(turn)
                mix_s[j, :, 128:256] = rhs3(mixer)
                if it == 0:
                    evo, tall = rows_of(j)
                    evos[j] = evo
                    talls[j] = tall
                    at_s[1, j] = (evo + dss[j]) * a_rows[j : j + 1]
                step = turn + (eye - mixer)
                guu = jnp.concatenate([sall[it, 2 * j, 0], sall[it, 2 * j + 1, 0]], axis=0)
                gtu = jnp.concatenate([sall[it, 2 * j, 1], sall[it, 2 * j + 1, 1]], axis=0)
                side = gtu + 0.5 * mm(grams[j], step)
                fresh.append(guu + narrow(gram_of([step, side], [side, step])))
            if it == 0:
                halo_send(at_s.at[1], hal_t.at[1], ht_s, ht_r.at[1])
            grams = fresh

    for ref, ssem, rsem in (
        (psend.at[pl.ds(0, 3)], px_s, px_r.at[0]),
        (ysend, py_s, py_r.at[0]),
        (fg.at[pl.ds(0, 7)], fg_s, fg_r),
        (gsend.at[pl.ds(0, 7)], g1_s, g1_r),
        (gall.at[pl.ds(0, 7)], g2_s, g2_r),
        (ssend.at[:, pl.ds(0, 7)], s1_s, s1_r.at[0]),
        (sall.at[:, pl.ds(0, 7)], s2_s, s2_r.at[0]),
        (qsend.at[pl.ds(0, 9)], q1_s, q1_r.at[0]),
        (zbuf.at[pl.ds(0, 21)], z_s, z_r.at[0]),
        (qall.at[pl.ds(0, 9)], q2_s, q2_r.at[0]),
        (hal_a, ha_s, ha_r.at[0]),
        (hal_t, ht_s, ht_r.at[0]),
        (hal_b, hb_s, hb_r),
    ):
        whole(ref, ssem, rsem).wait_send()


def body(data, order, chan_factor, slice_weights, smooth_aux, coupled, smooth_dual, coupling_dual, delta):
    vm = pltpu.VMEM
    dma = pltpu.SemaphoreType.DMA
    rows = (4, 48, 128)
    anyspace = pl.BlockSpec(memory_space=pl.ANY)
    vspace = pl.BlockSpec(memory_space=pltpu.VMEM)
    return pl.pallas_call(
        kernel,
        out_shape=(
            jax.ShapeDtypeStruct((8, 48, 64), F32),
            jax.ShapeDtypeStruct((8, 48, 64), F32),
            jax.ShapeDtypeStruct((64, 64), F32),
        ),
        in_specs=[pl.BlockSpec(memory_space=pltpu.SMEM)] + [anyspace] * 8,
        out_specs=(vspace, vspace, vspace),
        scratch_shapes=[
            vm((8, 384, 128), BF16), vm((64, 128), BF16), vm((8, 64), F32), vm((4, 8, 48, 64), F32), vm((64, 64), F32),
            vm((4, 4, 2, 48, 128), F32), vm((4, 4, 2, 48, 128), F32), vm(rows, F32), vm(rows, F32),
            vm((8, 32, 128), F32), vm((4, 64, 128), F32), vm((4, 64, 384), BF16), vm((4, 384, 128), BF16),
            vm((4, 64, 256), F32), vm((4, 64, 128), F32), vm((4, 64, 128), F32),
            vm((8, 32, 128), F32), vm((8, 32, 128), F32), vm((8, 32, 128), F32),
            vm((2, 8, 2, 32, 128), F32), vm((2, 8, 2, 32, 128), F32), vm((2, 8, 2, 32, 128), F32),
            vm((12, 8, 128), F32), vm((3, 4, 8, 128), F32), vm((24, 8, 128), F32), vm((12, 8, 128), F32),
            vm((2,) + rows, F32), vm(rows, F32), vm(rows, F32), vm(rows, F32), vm(rows, F32), vm((4, 384, 256), BF16),
            vm((2,) + rows, F32), vm(rows, F32),
            vm((2, 2) + rows, F32), vm((2, 2) + rows, F32), vm((8, 128), F32), vm((2, 8, 128), F32),
            dma((5,)), dma, dma((4,)), dma, dma((4,)), dma, dma, dma, dma, dma, dma, dma, dma((2,)), dma, dma((2,)),
            dma, dma((3,)), dma, dma((3,)), dma, dma((3,)), dma, dma((2,)), dma, dma((2,)), dma, dma,
        ],
        compiler_params=pltpu.CompilerParams(
            collective_id=0, has_side_effects=True, vmem_limit_bytes=60 * 1024 * 1024
        ),
    )(order, data, chan_factor.T, slice_weights, smooth_aux, coupled, smooth_dual, coupling_dual, delta)


def solution(mesh):
    return jax.shard_map(
        body,
        mesh=mesh,
        in_specs=(
            P("cuts", None, "chan"),
            P("cuts"),
            P("chan", None),
            P("cuts", None),
            P("cuts", "chan", None),
            P("cuts", "chan", None),
            P("cuts", "chan", None),
            P("cuts", "chan", None),
            P(),
        ),
        out_specs=(P("cuts", "chan", None), P("cuts", "chan", None), P()),
        check_vma=False,
    )
```

```python
import jax
import jax.numpy as jnp
from jax import lax
from jax.experimental import pallas as pl
from jax.experimental.pallas import tpu as pltpu
from jax.sharding import PartitionSpec as P

INNER = 3
POLAR = 8
NEWTON = 7
EPS_TRACE = 1e-06
F32 = jnp.float32
MESH = pl.DeviceIdType.MESH
CHEB_A = 0.1328125 / 1.2578125
CHEB_B = -1.0 / (512.0 * 1.2578125)


BF16 = jnp.bfloat16


def split(a):
    high = a.astype(BF16)
    return high, (a - high.astype(F32)).astype(BF16)


def lhs3(a):
    high, rest = split(a)
    return jnp.concatenate([high, rest, high], axis=1)


def dot(a, b):
    return jnp.dot(a, b, preferred_element_type=F32)


def gram_of(a, b):
    left, right = [], []
    for p, q in zip(a, b):
        ph, pl_ = split(p)
        qh, ql = split(q)
        left += [ph, pl_, ph]
        right += [qh, qh, ql]
    return lax.dot_general(
        jnp.concatenate(left, axis=0), jnp.concatenate(right, axis=0), (((0,), (0,)), ((), ())),
        preferred_element_type=F32,
    )


def kernel(
    order, data_h, fac_h, w_h, aux_h, coup_h, ds_h, dc_h, delta_h,
    evo_o, coup_o, delta_o,
    data_v, fac_v, w_v, rows_v, delta_v,
    psend, precv, ysend, yrecv, fg, x_s, sys_s, x_rhs, cr, left_s, k_s,
    gsend, grecv, gall, ssend, srecv, sall, qsend, qrecv, zbuf, qall,
    aux_p, dss, talls, evos, us, mix_s, at_s, baux, hal_a, hal_t, bsend, hal_b,
    load_sem, px_s, px_r, py_s, py_r, fg_s, fg_r, g1_s, g1_r, g2_s, g2_r, s1_s, s1_r, s2_s, s2_r,
    q1_s, q1_r, z_s, z_r, q2_s, q2_r, ha_s, ha_r, ht_s, ht_r, hb_s, hb_r,
):
    cuts = lax.axis_index("cuts")
    chan = lax.axis_index("chan")
    core = lax.rem(cuts, 2)
    zz = lax.rem(cuts // 2, 8)
    ylo = cuts // 16
    quad = ylo * 2 + core
    xx = lax.rem(chan, 4)
    yhi = chan // 4
    left_id = lax.rem(cuts + 31, 32)
    right_id = lax.rem(cuts + 1, 32)

    def z_dev(z):
        return (ylo * 16 + z * 2 + core, chan)

    def quad_dev(q):
        return ((q // 2) * 16 + zz * 2 + lax.rem(q, 2), chan)

    def send(src, dst, ssem, rsem, dev):
        pltpu.make_async_remote_copy(
            src_ref=src, dst_ref=dst, send_sem=ssem, recv_sem=rsem, device_id=dev, device_id_type=MESH
        ).start()

    def whole(ref, ssem, rsem):
        return pltpu.make_async_remote_copy(
            src_ref=ref, dst_ref=ref, send_sem=ssem, recv_sem=rsem, device_id=(left_id, chan), device_id_type=MESH
        )

    def arrived(ref, ssem, rsem):
        whole(ref, ssem, rsem).wait_recv()

    def load(src, dst, n):
        return pltpu.make_async_copy(src, dst, load_sem.at[n])

    load(fac_h, fac_v, 0).start()
    load(data_h, data_v, 1).start()
    load(w_h, w_v, 2).start()
    for n, src in enumerate((aux_h, coup_h, ds_h, dc_h)):
        load(src, rows_v.at[n], 3).start()
    load(delta_h, delta_v, 4).start()

    barrier = pltpu.get_barrier_semaphore()
    greet = [(cuts, lax.rem(chan + d, 8)) for d in range(1, 8)]
    greet += [z_dev(lax.rem(zz + d, 8)) for d in range(1, 8)]
    greet += [quad_dev(lax.rem(quad + d, 4)) for d in range(1, 4)]
    greet += [(left_id, chan), (right_id, chan)]
    for dev in greet:
        pl.semaphore_signal(barrier, inc=1, device_id=dev, device_id_type=MESH)

    lane = lax.broadcasted_iota(jnp.int32, (1, 128), 1)
    low = lane < 64
    high = lane >= 64
    row_i = lax.broadcasted_iota(jnp.int32, (64, 128), 0)
    col_i = lax.broadcasted_iota(jnp.int32, (64, 128), 1)
    eye_b = row_i == lax.rem(col_i, 64)
    eye = eye_b.astype(F32)
    low16 = low.astype(F32).astype(BF16)
    high16 = high.astype(F32).astype(BF16)

    def swap(v):
        return pltpu.roll(v, 64, 1)

    def widen(v):
        return jnp.concatenate([v * low16, v * high16], axis=0)

    def rhs3(a):
        first, rest = split(a)
        first, rest = widen(first), widen(rest)
        return jnp.concatenate([first, first, rest], axis=0)

    def mm(a, b):
        return dot(lhs3(a), rhs3(b))

    def narrow(t):
        return jnp.where(low, t[0:64], t[64:128])

    def unpack(p):
        q = swap(p)
        return jnp.concatenate([jnp.where(low, p, q), jnp.where(low, q, p)], axis=0)

    def transposed(c):
        return jnp.concatenate([c, c], axis=0).T[0:64]

    def half_sums(v):
        zero = jnp.zeros_like(v)
        lo = jnp.sum(jnp.where(low, v, zero), axis=1, keepdims=True)
        hi = jnp.sum(jnp.where(low, zero, v), axis=1, keepdims=True)
        return jnp.where(low, lo, hi)

    load(fac_h, fac_v, 0).wait()
    fac = fac_v[...]
    nt = (((1,), (1,)), ((), ()))
    partial_gram = lax.dot_general(fac, fac, nt, preferred_element_type=F32)
    fg[chan] = jnp.concatenate([partial_gram[0:32], partial_gram[32:64]], axis=1)
    zero_fac = jnp.zeros_like(fac)
    fac2 = jnp.concatenate(
        [jnp.concatenate([fac, zero_fac], axis=1), jnp.concatenate([zero_fac, fac], axis=1)], axis=0
    )
    load(data_h, data_v, 1).wait()
    for j in range(4):
        first = data_v[lax.rem(order[j], 8)]
        second = data_v[lax.rem(order[j + 4], 8)]
        out = lax.dot_general(jnp.concatenate([first, second], axis=1), fac2, nt, preferred_element_type=F32)
        for c in range(8):
            psend[j, c % 4, c // 4] = out[48 * c : 48 * c + 48]
    pl.semaphore_wait(barrier, len(greet))
    for d in range(1, 8):
        peer = lax.rem(chan + d, 8)
        send(fg.at[chan], fg.at[chan], fg_s, fg_r, (cuts, peer))
    for j in range(4):
        for d in (2, 1, 3):
            to = lax.rem(xx + d, 4)
            send(psend.at[j, to], precv.at[j, xx], px_s, px_r.at[j], (cuts, yhi * 4 + to))

    load(w_h, w_v, 2).wait()
    load(rows_v, rows_v, 3).wait()
    load(delta_h, delta_v, 4).wait()

    def pair(n, j):
        return jnp.concatenate([rows_v[n, j], rows_v[n, j + 4]], axis=1)

    for j in range(4):
        aux_p[0, j] = pair(0, j)
        dss[j] = pair(2, j)
        dual = pair(3, j)
        talls[j] = dual
        us[j] = pair(1, j) - dual

    def halo_send(src, dst, ssem, rsem):
        send(src, dst.at[0], ssem, rsem, (right_id, chan))
        send(src, dst.at[1], ssem, rsem, (left_id, chan))

    halo_send(aux_p.at[0], hal_a.at[0], ha_s, ha_r.at[0])

    arrived(fg.at[pl.ds(0, 7)], fg_s, fg_r)
    gram_sum = fg[0]
    for c in range(1, 8):
        gram_sum = gram_sum + fg[c]
    gram2 = unpack(gram_sum)
    w = w_v[...]
    w2 = jnp.concatenate([w[0:4], w[4:8]], axis=1)
    diag_row = jnp.sum(jnp.where(eye_b, gram2, 0.0), axis=0, keepdims=True)
    rho = half_sums(w2 * w2 * diag_row) * (1.0 / 64.0)
    w_over = w2 / rho
    b_rows = 2.0 / (rho + 4.0)
    a_rows = rho / (rho + 4.0)
    bsend[0:4] = b_rows
    bsend[4:8] = b_rows
    halo_send(bsend, hal_b, hb_s, hb_r)
    for j in range(4):
        w_col = half_sums(jnp.where(eye_b, w2[j : j + 1], 0.0))
        system = gram2 * w_col * w_over[j : j + 1] + 2.0 * eye
        sys_s[j] = lhs3(system)
        x_s[j] = CHEB_A * eye + CHEB_B * system

    def newton(step, carry):
        xs = [x_s[j] for j in range(4)]
        gaps = [2.0 * eye - dot(sys_s[j], rhs3(xs[j])) for j in range(4)]
        fresh = [mm(xs[j], gaps[j]) for j in range(4)]
        for j in range(4):
            x_s[j] = fresh[j]
        return carry

    def forward(j):
        arrived(precv.at[j, pl.ds(0, 3)], px_s, px_r.at[j])
        total = psend[j, xx, 1 - yhi]
        for d in range(1, 4):
            total = total + precv[j, lax.rem(xx + d, 4), 1 - yhi]
        ysend[j] = total
        send(ysend.at[j], yrecv.at[j], py_s, py_r.at[j], (cuts, (1 - yhi) * 4 + xx))
        total = psend[j, xx, yhi]
        for d in range(1, 4):
            total = total + precv[j, lax.rem(xx + d, 4), yhi]
        baux[j] = total

    lax.fori_loop(0, 2, newton, 0)
    forward(0)
    lax.fori_loop(0, 3, newton, 0)
    forward(1)
    lax.fori_loop(0, NEWTON - 5, newton, 0)
    forward(2)
    for j in range(4):
        x_rhs[j] = rhs3(x_s[j])
    forward(3)

    delta_in = delta_v[...]
    delta = jnp.concatenate([delta_in, delta_in], axis=1)

    def spread(buf, ssem, rsem, own):
        buf[chan] = own
        for d in range(1, 8):
            send(buf.at[chan], buf.at[chan], ssem, rsem, (cuts, lax.rem(chan + d, 8)))

    def scatter(src, dst, ssem, rsem):
        for d in range(1, 8):
            peer = lax.rem(chan + d, 8)
            send(src.at[peer], dst.at[chan], ssem, rsem, (cuts, peer))
        dst[chan] = src[chan]

    def from_chan(buf, ssem, rsem):
        arrived(buf.at[pl.ds(0, 7)], ssem, rsem)

    def total_of(buf):
        total = buf[0]
        for c in range(1, 8):
            total = total + buf[c]
        return total

    def smooth(it):
        arrived(hal_a.at[it], ha_s, ha_r.at[it])
        arrived(hal_t.at[it], ht_s, ht_r.at[it])
        if it == 0:
            arrived(hal_b, hb_s, hb_r)
        vals, tars, bs = [], [], []
        for p in range(4):
            vals.append(jnp.where(low, swap(hal_a[it, 0, p]), aux_p[it, p]))
            tars.append(jnp.where(low, swap(hal_t[it, 0, p]), at_s[it, p]))
            bs.append(jnp.where(low, swap(hal_b[0, p : p + 1]), bsend[p : p + 1]))
        for p in range(4):
            vals.append(jnp.where(low, aux_p[it, p], swap(hal_a[it, 1, p])))
            tars.append(jnp.where(low, at_s[it, p], swap(hal_t[it, 1, p])))
            bs.append(jnp.where(low, bsend[p : p + 1], swap(hal_b[1, p : p + 1])))
        for sweep in range(4):
            fresh = []
            for p in range(8):
                before = vals[p - 1] if p > 0 else swap(vals[7])
                after = vals[p + 1] if p < 7 else swap(vals[0])
                fresh.append(tars[p] + bs[p] * (before + after))
            vals = fresh
        for j in range(4):
            aux = jnp.where(low, vals[4 + j], vals[j])
            dual = dss[j] + evos[j] - aux
            if it == 0:
                aux_p[1, j] = aux
            dss[j] = dual
            us[j] = dot(lhs3(baux[j] + (aux - dual)), x_rhs[j])
        if it == 0:
            halo_send(aux_p.at[1], hal_a.at[1], ha_s, ha_r.at[1])
        for j in range(4):
            u, tall = us[j], talls[j]
            guu = narrow(gram_of([u], [u]))
            gtu = narrow(gram_of([tall], [u]))
            for h in range(2):
                ssend[it, 2 * j + h, 0] = guu[32 * h : 32 * h + 32]
                ssend[it, 2 * j + h, 1] = gtu[32 * h : 32 * h + 32]
        scatter(ssend.at[it], srecv.at[it], s1_s, s1_r.at[it])

    def gather_sums(it):
        from_chan(srecv.at[it], s1_s, s1_r.at[it])
        spread(sall.at[it], s2_s, s2_r.at[it], total_of(srecv.at[it]))

    def rows_of(j):
        tall = talls[j]
        both = dot(lhs3(tall), mix_s[j])
        evo = us[j] + both[:, 0:128]
        return evo, evo + (tall - both[:, 128:256])

    def polar(step, carry):
        for j in range(4):
            both = cr[j]
            root = both[:, 128:256]
            ch, cl = split(both[:, 0:128])
            rh, rl = split(root)
            ch, cl = widen(ch), widen(cl)
            prod = dot(lhs3(root), jnp.concatenate([ch, ch, cl], axis=0))
            firsts = jnp.concatenate([ch, widen(rh)], axis=1)
            rests = jnp.concatenate([cl, widen(rl)], axis=1)
            bracket = 1.5 * eye - 0.5 * prod
            cr[j] = dot(lhs3(bracket), jnp.concatenate([firsts, firsts, rests], axis=0))
        return carry

    fresh = []
    for j in range(4):
        arrived(yrecv.at[j], py_s, py_r.at[j])
        baux[j] = (baux[j] + yrecv[j]) * w_over[j : j + 1]
        fresh.append(dot(lhs3(baux[j] + (aux_p[0, j] - dss[j]) + us[j]), x_rhs[j]))
    for j in range(4):
        tall = fresh[j] + talls[j]
        evos[j] = fresh[j]
        talls[j] = tall
        part = narrow(gram_of([tall], [tall]))
        gsend[2 * j] = part[0:32]
        gsend[2 * j + 1] = part[32:64]
    scatter(gsend, grecv, g1_s, g1_r)
    for j in range(4):
        at_s[0, j] = (evos[j] + dss[j]) * a_rows[j : j + 1]
    halo_send(at_s.at[0], hal_t.at[0], ht_s, ht_r.at[0])
    from_chan(grecv, g1_s, g1_r)
    spread(gall, g2_s, g2_r, total_of(grecv))
    smooth(0)
    from_chan(gall, g2_s, g2_r)
    grams = [jnp.concatenate([gall[2 * j], gall[2 * j + 1]], axis=0) for j in range(4)]

    for it in range(INNER):
        last = it == INNER - 1
        delta_t = transposed(delta)
        delta_l = lhs3(delta)
        delta_r = rhs3(delta_t)
        lefts = [dot(delta_l, rhs3(grams[j])) for j in range(4)]
        normals = [dot(lhs3(lefts[j]), delta_r) for j in range(4)]
        scales, curs, brackets = [], [], []
        for j in range(4):
            left_s[j] = lefts[j]
            trace = half_sums(jnp.sum(jnp.where(eye_b, normals[j], 0.0), axis=0, keepdims=True)) + EPS_TRACE
            scales.append(1.0 / jnp.sqrt(trace))
            curs.append(normals[j] * (1.0 / trace))
            brackets.append(1.5 * eye - 0.5 * curs[j])
        firsts = [mm(brackets[j], curs[j]) for j in range(4)]
        for j in range(4):
            cr[j, :, 0:128] = firsts[j]
            cr[j, :, 128:256] = brackets[j]

        if it == 0:
            lax.fori_loop(0, 3, polar, 0)
            gather_sums(0)
            lax.fori_loop(0, POLAR - 5, polar, 0)
        elif it == 1:
            lax.fori_loop(0, 2, polar, 0)
            smooth(1)
            lax.fori_loop(0, POLAR - 4, polar, 0)
        else:
            lax.fori_loop(0, POLAR - 2, polar, 0)
        boths = [cr[j] for j in range(4)]
        prods = [mm(boths[j][:, 128:256], boths[j][:, 0:128]) for j in range(4)]
        roots = [mm(1.5 * eye - 0.5 * prods[j], boths[j][:, 128:256]) for j in range(4)]
        parts = [mm(roots[j], left_s[j]) * scales[j] for j in range(4)]
        for j in range(4):
            k_s[j] = roots[j]
        part = (parts[0] + parts[1]) + (parts[2] + parts[3])
        part = part + swap(part)
        packed = jnp.where(low, part[0:32], part[32:64])
        for q in range(4):
            qsend[it * 4 + q] = packed[8 * q : 8 * q + 8]
        for d in range(1, 4):
            to = lax.rem(quad + d, 4)
            send(qsend.at[it * 4 + to], qrecv.at[it, quad], q1_s, q1_r.at[it], quad_dev(to))
        qrecv[it, quad] = qsend[it * 4 + quad]
        if it == 1:
            gather_sums(1)
        delta_tl = lhs3(delta_t)
        for j in range(4):
            k_s[j] = dot(delta_tl, rhs3(k_s[j])) * scales[j]
        arrived(qrecv.at[it, pl.ds(0, 3)], q1_s, q1_r.at[it])
        zbuf[it * 8 + zz] = (qrecv[it, 0] + qrecv[it, 1]) + (qrecv[it, 2] + qrecv[it, 3])
        for d in (4, 3, 5, 2, 6, 1, 7):
            slot = zbuf.at[it * 8 + zz]
            send(slot, slot, z_s, z_r.at[it], z_dev(lax.rem(zz + d, 8)))
        if last:
            for j in range(4):
                evo, tall = rows_of(j)
                talls[j] = tall
                evo_o[j] = evo[:, 0:64]
                evo_o[j + 4] = evo[:, 64:128]
        arrived(zbuf.at[pl.ds(it * 8, 7)], z_s, z_r.at[it])
        total = zbuf[it * 8]
        for z in range(1, 8):
            total = total + zbuf[it * 8 + z]
        qall[it * 4 + quad] = total * (1.0 / 256.0)
        for d in range(1, 4):
            slot = qall.at[it * 4 + quad]
            send(slot, slot, q2_s, q2_r.at[it], quad_dev(lax.rem(quad + d, 4)))
        if not last:
            from_chan(sall.at[it], s2_s, s2_r.at[it])
        arrived(qall.at[pl.ds(it * 4, 3)], q2_s, q2_r.at[it])
        delta = unpack(jnp.concatenate([qall[it * 4 + q] for q in range(4)], axis=0))
        fresh_r = rhs3(delta)

        if last:
            mixers = [dot(lhs3(k_s[j]), fresh_r) for j in range(4)]
            coups = [mm(talls[j], mixers[j]) for j in range(4)]
            for j in range(4):
                coup_o[j] = coups[j][:, 0:64]
                coup_o[j + 4] = coups[j][:, 64:128]
            delta_o[...] = delta[:, 0:64]
        else:
            mixers = [dot(lhs3(k_s[j]), fresh_r) for j in range(4)]
            turns = [dot(lhs3(2.0 * mixers[j] - eye), x_rhs[j]) for j in range(4)]
            for j in range(4):
                mix_s[j, :, 0:128] = rhs3(turns[j])
                mix_s[j, :, 128:256] = rhs3(mixers[j])
            steps = [turns[j] + (eye - mixers[j]) for j in range(4)]
            sides = [mm(grams[j], steps[j]) for j in range(4)]
            if it == 0:
                fresh = [rows_of(j) for j in range(4)]
                for j in range(4):
                    evos[j], talls[j] = fresh[j]
                    at_s[1, j] = (fresh[j][0] + dss[j]) * a_rows[j : j + 1]
            grams = []
            for j in range(4):
                guu = jnp.concatenate([sall[it, 2 * j, 0], sall[it, 2 * j + 1, 0]], axis=0)
                gtu = jnp.concatenate([sall[it, 2 * j, 1], sall[it, 2 * j + 1, 1]], axis=0)
                side = gtu + 0.5 * sides[j]
                grams.append(guu + narrow(gram_of([steps[j], side], [side, steps[j]])))
            if it == 0:
                halo_send(at_s.at[1], hal_t.at[1], ht_s, ht_r.at[1])

    for ref, ssem, rsem in (
        (psend.at[pl.ds(0, 3)], px_s, px_r.at[0]),
        (ysend, py_s, py_r.at[0]),
        (fg.at[pl.ds(0, 7)], fg_s, fg_r),
        (gsend.at[pl.ds(0, 7)], g1_s, g1_r),
        (gall.at[pl.ds(0, 7)], g2_s, g2_r),
        (ssend.at[:, pl.ds(0, 7)], s1_s, s1_r.at[0]),
        (sall.at[:, pl.ds(0, 7)], s2_s, s2_r.at[0]),
        (qsend.at[pl.ds(0, 9)], q1_s, q1_r.at[0]),
        (zbuf.at[pl.ds(0, 21)], z_s, z_r.at[0]),
        (qall.at[pl.ds(0, 9)], q2_s, q2_r.at[0]),
        (hal_a, ha_s, ha_r.at[0]),
        (hal_t, ht_s, ht_r.at[0]),
        (hal_b, hb_s, hb_r),
    ):
        whole(ref, ssem, rsem).wait_send()


def body(data, order, chan_factor, slice_weights, smooth_aux, coupled, smooth_dual, coupling_dual, delta):
    vm = pltpu.VMEM
    dma = pltpu.SemaphoreType.DMA
    rows = (4, 48, 128)
    anyspace = pl.BlockSpec(memory_space=pl.ANY)
    vspace = pl.BlockSpec(memory_space=pltpu.VMEM)
    return pl.pallas_call(
        kernel,
        out_shape=(
            jax.ShapeDtypeStruct((8, 48, 64), F32),
            jax.ShapeDtypeStruct((8, 48, 64), F32),
            jax.ShapeDtypeStruct((64, 64), F32),
        ),
        in_specs=[pl.BlockSpec(memory_space=pltpu.SMEM)] + [anyspace] * 8,
        out_specs=(vspace, vspace, vspace),
        scratch_shapes=[
            vm((8, 384, 128), BF16), vm((64, 128), BF16), vm((8, 64), F32), vm((4, 8, 48, 64), F32), vm((64, 64), F32),
            vm((4, 4, 2, 48, 128), F32), vm((4, 4, 2, 48, 128), F32), vm(rows, F32), vm(rows, F32),
            vm((8, 32, 128), F32), vm((4, 64, 128), F32), vm((4, 64, 384), BF16), vm((4, 384, 128), BF16),
            vm((4, 64, 256), F32), vm((4, 64, 128), F32), vm((4, 64, 128), F32),
            vm((8, 32, 128), F32), vm((8, 32, 128), F32), vm((8, 32, 128), F32),
            vm((2, 8, 2, 32, 128), F32), vm((2, 8, 2, 32, 128), F32), vm((2, 8, 2, 32, 128), F32),
            vm((12, 8, 128), F32), vm((3, 4, 8, 128), F32), vm((24, 8, 128), F32), vm((12, 8, 128), F32),
            vm((2,) + rows, F32), vm(rows, F32), vm(rows, F32), vm(rows, F32), vm(rows, F32), vm((4, 384, 256), BF16),
            vm((2,) + rows, F32), vm(rows, F32),
            vm((2, 2) + rows, F32), vm((2, 2) + rows, F32), vm((8, 128), F32), vm((2, 8, 128), F32),
            dma((5,)), dma, dma((4,)), dma, dma((4,)), dma, dma, dma, dma, dma, dma, dma, dma((2,)), dma, dma((2,)),
            dma, dma((3,)), dma, dma((3,)), dma, dma((3,)), dma, dma((2,)), dma, dma((2,)), dma, dma,
        ],
        compiler_params=pltpu.CompilerParams(
            collective_id=0, has_side_effects=True, vmem_limit_bytes=60 * 1024 * 1024
        ),
    )(order, data, chan_factor.T, slice_weights, smooth_aux, coupled, smooth_dual, coupling_dual, delta)


def solution(mesh):
    return jax.shard_map(
        body,
        mesh=mesh,
        in_specs=(
            P("cuts", None, "chan"),
            P("cuts"),
            P("chan", None),
            P("cuts", None),
            P("cuts", "chan", None),
            P("cuts", "chan", None),
            P("cuts", "chan", None),
            P("cuts", "chan", None),
            P(),
        ),
        out_specs=(P("cuts", "chan", None), P("cuts", "chan", None), P()),
        check_vma=False,
    )
```

```python
import jax
import jax.numpy as jnp
from jax import lax
from jax.experimental import pallas as pl
from jax.experimental.pallas import tpu as pltpu
from jax.sharding import PartitionSpec as P

INNER = 3
POLAR = 8
NEWTON = 7
EPS_TRACE = 1e-06
F32 = jnp.float32
MESH = pl.DeviceIdType.MESH
CHEB_A = 0.1328125 / 1.2578125
CHEB_B = -1.0 / (512.0 * 1.2578125)


BF16 = jnp.bfloat16


def split(a):
    high = a.astype(BF16)
    return high, (a - high.astype(F32)).astype(BF16)


def lhs3(a):
    high, rest = split(a)
    return jnp.concatenate([high, rest, high], axis=1)


def dot(a, b):
    return jnp.dot(a, b, preferred_element_type=F32)


def gram_of(a, b):
    left, right = [], []
    for p, q in zip(a, b):
        ph, pl_ = split(p)
        qh, ql = split(q)
        left += [ph, pl_, ph]
        right += [qh, qh, ql]
    return lax.dot_general(
        jnp.concatenate(left, axis=0), jnp.concatenate(right, axis=0), (((0,), (0,)), ((), ())),
        preferred_element_type=F32,
    )


def kernel(
    order, data_h, fac_h, w_h, aux_h, coup_h, ds_h, dc_h, delta_h,
    evo_o, coup_o, delta_o,
    data_v, fac_v, w_v, rows_v, delta_v,
    psend, precv, ysend, yrecv, fg, x_s, sys_s, x_rhs, cr, left_s, k_l, gram_l, gtu_s,
    gsend, grecv, gall, ssend, srecv, sall, qsend, qrecv, zbuf, qall,
    aux_p, dss, talls, evos, us, mix_s, at_s, baux, hal_a, hal_t, bsend, hal_b,
    load_sem, px_s, px_r, py_s, py_r, fg_s, fg_r, g1_s, g1_r, g2_s, g2_r, s1_s, s1_r, s2_s, s2_r,
    q1_s, q1_r, z_s, z_r, q2_s, q2_r, ha_s, ha_r, ht_s, ht_r, hb_s, hb_r,
):
    cuts = lax.axis_index("cuts")
    chan = lax.axis_index("chan")
    core = lax.rem(cuts, 2)
    zz = lax.rem(cuts // 2, 8)
    ylo = cuts // 16
    quad = ylo * 2 + core
    xx = lax.rem(chan, 4)
    yhi = chan // 4
    left_id = lax.rem(cuts + 31, 32)
    right_id = lax.rem(cuts + 1, 32)

    def z_dev(z):
        return (ylo * 16 + z * 2 + core, chan)

    def quad_dev(q):
        return ((q // 2) * 16 + zz * 2 + lax.rem(q, 2), chan)

    def send(src, dst, ssem, rsem, dev):
        pltpu.make_async_remote_copy(
            src_ref=src, dst_ref=dst, send_sem=ssem, recv_sem=rsem, device_id=dev, device_id_type=MESH
        ).start()

    def whole(ref, ssem, rsem):
        return pltpu.make_async_remote_copy(
            src_ref=ref, dst_ref=ref, send_sem=ssem, recv_sem=rsem, device_id=(left_id, chan), device_id_type=MESH
        )

    def arrived(ref, ssem, rsem):
        whole(ref, ssem, rsem).wait_recv()

    def load(src, dst, n):
        return pltpu.make_async_copy(src, dst, load_sem.at[n])

    load(fac_h, fac_v, 0).start()
    load(data_h, data_v, 1).start()
    load(w_h, w_v, 2).start()
    for n, src in enumerate((aux_h, coup_h, ds_h, dc_h)):
        load(src, rows_v.at[n], 3).start()
    load(delta_h, delta_v, 4).start()

    barrier = pltpu.get_barrier_semaphore()
    greet = [(cuts, lax.rem(chan + d, 8)) for d in range(1, 8)]
    greet += [z_dev(lax.rem(zz + d, 8)) for d in range(1, 8)]
    greet += [quad_dev(lax.rem(quad + d, 4)) for d in range(1, 4)]
    greet += [(left_id, chan), (right_id, chan)]
    for dev in greet:
        pl.semaphore_signal(barrier, inc=1, device_id=dev, device_id_type=MESH)

    lane = lax.broadcasted_iota(jnp.int32, (1, 128), 1)
    low = lane < 64
    high = lane >= 64
    row_i = lax.broadcasted_iota(jnp.int32, (64, 128), 0)
    col_i = lax.broadcasted_iota(jnp.int32, (64, 128), 1)
    eye_b = row_i == lax.rem(col_i, 64)
    eye = eye_b.astype(F32)
    low16 = low.astype(F32).astype(BF16)
    high16 = high.astype(F32).astype(BF16)

    def swap(v):
        return pltpu.roll(v, 64, 1)

    def widen(v):
        return jnp.concatenate([v * low16, v * high16], axis=0)

    def rhs3(a):
        first, rest = split(a)
        first, rest = widen(first), widen(rest)
        return jnp.concatenate([first, first, rest], axis=0)

    def mm(a, b):
        return dot(lhs3(a), rhs3(b))

    def narrow(t):
        return jnp.where(low, t[0:64], t[64:128])

    def unpack(p):
        q = swap(p)
        return jnp.concatenate([jnp.where(low, p, q), jnp.where(low, q, p)], axis=0)

    def transposed(c):
        return jnp.concatenate([c, c], axis=0).T[0:64]

    def half_sums(v):
        zero = jnp.zeros_like(v)
        lo = jnp.sum(jnp.where(low, v, zero), axis=1, keepdims=True)
        hi = jnp.sum(jnp.where(low, zero, v), axis=1, keepdims=True)
        return jnp.where(low, lo, hi)

    load(fac_h, fac_v, 0).wait()
    fac = fac_v[...]
    nt = (((1,), (1,)), ((), ()))
    partial_gram = lax.dot_general(fac, fac, nt, preferred_element_type=F32)
    fg[chan] = jnp.concatenate([partial_gram[0:32], partial_gram[32:64]], axis=1)
    zero_fac = jnp.zeros_like(fac)
    fac2 = jnp.concatenate(
        [jnp.concatenate([fac, zero_fac], axis=1), jnp.concatenate([zero_fac, fac], axis=1)], axis=0
    )
    load(data_h, data_v, 1).wait()
    for j in range(4):
        first = data_v[lax.rem(order[j], 8)]
        second = data_v[lax.rem(order[j + 4], 8)]
        out = lax.dot_general(jnp.concatenate([first, second], axis=1), fac2, nt, preferred_element_type=F32)
        for c in range(8):
            psend[j, c % 4, c // 4] = out[48 * c : 48 * c + 48]
    pl.semaphore_wait(barrier, len(greet))
    for d in range(1, 8):
        peer = lax.rem(chan + d, 8)
        send(fg.at[chan], fg.at[chan], fg_s, fg_r, (cuts, peer))
    for j in range(4):
        for d in (2, 1, 3):
            to = lax.rem(xx + d, 4)
            send(psend.at[j, to], precv.at[j, xx], px_s, px_r.at[j], (cuts, yhi * 4 + to))

    load(w_h, w_v, 2).wait()
    load(rows_v, rows_v, 3).wait()
    load(delta_h, delta_v, 4).wait()

    def pair(n, j):
        return jnp.concatenate([rows_v[n, j], rows_v[n, j + 4]], axis=1)

    for j in range(4):
        aux_p[0, j] = pair(0, j)
        dss[j] = pair(2, j)
        dual = pair(3, j)
        talls[j] = dual
        us[j] = pair(1, j) - dual

    def halo_send(src, dst, ssem, rsem):
        send(src, dst.at[0], ssem, rsem, (right_id, chan))
        send(src, dst.at[1], ssem, rsem, (left_id, chan))

    halo_send(aux_p.at[0], hal_a.at[0], ha_s, ha_r.at[0])

    arrived(fg.at[pl.ds(0, 7)], fg_s, fg_r)
    gram_sum = fg[0]
    for c in range(1, 8):
        gram_sum = gram_sum + fg[c]
    gram2 = unpack(gram_sum)
    w = w_v[...]
    w2 = jnp.concatenate([w[0:4], w[4:8]], axis=1)
    diag_row = jnp.sum(jnp.where(eye_b, gram2, 0.0), axis=0, keepdims=True)
    rho = half_sums(w2 * w2 * diag_row) * (1.0 / 64.0)
    w_over = w2 / rho
    b_rows = 2.0 / (rho + 4.0)
    a_rows = rho / (rho + 4.0)
    bsend[0:4] = b_rows
    bsend[4:8] = b_rows
    halo_send(bsend, hal_b, hb_s, hb_r)
    for j in range(4):
        w_col = half_sums(jnp.where(eye_b, w2[j : j + 1], 0.0))
        system = gram2 * w_col * w_over[j : j + 1] + 2.0 * eye
        sys_s[j] = lhs3(system)
        x_s[j] = CHEB_A * eye + CHEB_B * system

    def newton(step, carry):
        xs = [x_s[j] for j in range(4)]
        gaps = [2.0 * eye - dot(sys_s[j], rhs3(xs[j])) for j in range(4)]
        fresh = [mm(xs[j], gaps[j]) for j in range(4)]
        for j in range(4):
            x_s[j] = fresh[j]
        return carry

    def forward(j):
        arrived(precv.at[j, pl.ds(0, 3)], px_s, px_r.at[j])
        total = psend[j, xx, 1 - yhi]
        for d in range(1, 4):
            total = total + precv[j, lax.rem(xx + d, 4), 1 - yhi]
        ysend[j] = total
        send(ysend.at[j], yrecv.at[j], py_s, py_r.at[j], (cuts, (1 - yhi) * 4 + xx))
        total = psend[j, xx, yhi]
        for d in range(1, 4):
            total = total + precv[j, lax.rem(xx + d, 4), yhi]
        baux[j] = total

    lax.fori_loop(0, 2, newton, 0)
    forward(0)
    lax.fori_loop(0, 3, newton, 0)
    forward(1)
    lax.fori_loop(0, NEWTON - 5, newton, 0)
    forward(2)
    for j in range(4):
        x_rhs[j] = rhs3(x_s[j])
    forward(3)

    delta_in = delta_v[...]
    delta = jnp.concatenate([delta_in, delta_in], axis=1)

    def spread(buf, ssem, rsem, own):
        buf[chan] = own
        for d in range(1, 8):
            send(buf.at[chan], buf.at[chan], ssem, rsem, (cuts, lax.rem(chan + d, 8)))

    def scatter(src, dst, ssem, rsem):
        for d in range(1, 8):
            peer = lax.rem(chan + d, 8)
            send(src.at[peer], dst.at[chan], ssem, rsem, (cuts, peer))
        dst[chan] = src[chan]

    def from_chan(buf, ssem, rsem):
        arrived(buf.at[pl.ds(0, 7)], ssem, rsem)

    def total_of(buf):
        total = buf[0]
        for c in range(1, 8):
            total = total + buf[c]
        return total

    def smooth(it):
        arrived(hal_a.at[it], ha_s, ha_r.at[it])
        arrived(hal_t.at[it], ht_s, ht_r.at[it])
        if it == 0:
            arrived(hal_b, hb_s, hb_r)
        vals, tars, bs = [], [], []
        for p in range(4):
            vals.append(jnp.where(low, swap(hal_a[it, 0, p]), aux_p[it, p]))
            tars.append(jnp.where(low, swap(hal_t[it, 0, p]), at_s[it, p]))
            bs.append(jnp.where(low, swap(hal_b[0, p : p + 1]), bsend[p : p + 1]))
        for p in range(4):
            vals.append(jnp.where(low, aux_p[it, p], swap(hal_a[it, 1, p])))
            tars.append(jnp.where(low, at_s[it, p], swap(hal_t[it, 1, p])))
            bs.append(jnp.where(low, bsend[p : p + 1], swap(hal_b[1, p : p + 1])))
        for sweep in range(4):
            fresh = []
            for p in range(8):
                before = vals[p - 1] if p > 0 else swap(vals[7])
                after = vals[p + 1] if p < 7 else swap(vals[0])
                fresh.append(tars[p] + bs[p] * (before + after))
            vals = fresh
        for j in range(4):
            aux = jnp.where(low, vals[4 + j], vals[j])
            dual = dss[j] + evos[j] - aux
            if it == 0:
                aux_p[1, j] = aux
            dss[j] = dual
            us[j] = dot(lhs3(baux[j] + (aux - dual)), x_rhs[j])
        if it == 0:
            halo_send(aux_p.at[1], hal_a.at[1], ha_s, ha_r.at[1])
        for j in range(4):
            u, tall = us[j], talls[j]
            sums = gram_of([u], [jnp.concatenate([u, tall], axis=1)])
            guu, gut = narrow(sums[:, 0:128]), narrow(sums[:, 128:256])
            for h in range(2):
                ssend[it, 2 * j + h, 0] = guu[32 * h : 32 * h + 32]
                ssend[it, 2 * j + h, 1] = gut[32 * h : 32 * h + 32]
        scatter(ssend.at[it], srecv.at[it], s1_s, s1_r.at[it])

    def gather_sums(it):
        from_chan(srecv.at[it], s1_s, s1_r.at[it])
        spread(sall.at[it], s2_s, s2_r.at[it], total_of(srecv.at[it]))

    def rows_of(j):
        tall = talls[j]
        both = dot(lhs3(tall), mix_s[j])
        evo = us[j] + both[:, 0:128]
        return evo, evo + (tall - both[:, 128:256])

    def polar(step, carry):
        for j in range(4):
            both = cr[j]
            root = both[:, 128:256]
            ch, cl = split(both[:, 0:128])
            rh, rl = split(root)
            ch, cl = widen(ch), widen(cl)
            prod = dot(lhs3(root), jnp.concatenate([ch, ch, cl], axis=0))
            firsts = jnp.concatenate([ch, widen(rh)], axis=1)
            rests = jnp.concatenate([cl, widen(rl)], axis=1)
            bracket = 1.5 * eye - 0.5 * prod
            cr[j] = dot(lhs3(bracket), jnp.concatenate([firsts, firsts, rests], axis=0))
        return carry

    fresh = []
    for j in range(4):
        arrived(yrecv.at[j], py_s, py_r.at[j])
        baux[j] = (baux[j] + yrecv[j]) * w_over[j : j + 1]
        fresh.append(dot(lhs3(baux[j] + (aux_p[0, j] - dss[j]) + us[j]), x_rhs[j]))
    for j in range(4):
        tall = fresh[j] + talls[j]
        evos[j] = fresh[j]
        talls[j] = tall
        part = narrow(gram_of([tall], [tall]))
        gsend[2 * j] = part[0:32]
        gsend[2 * j + 1] = part[32:64]
    scatter(gsend, grecv, g1_s, g1_r)
    for j in range(4):
        at_s[0, j] = (evos[j] + dss[j]) * a_rows[j : j + 1]
    halo_send(at_s.at[0], hal_t.at[0], ht_s, ht_r.at[0])
    from_chan(grecv, g1_s, g1_r)
    spread(gall, g2_s, g2_r, total_of(grecv))
    smooth(0)
    from_chan(gall, g2_s, g2_r)
    grams = [jnp.concatenate([gall[2 * j], gall[2 * j + 1]], axis=0) for j in range(4)]

    delta_t = transposed(delta)
    for it in range(INNER):
        last = it == INNER - 1
        delta_l = lhs3(delta)
        delta_r = rhs3(delta_t)
        lefts = [dot(delta_l, rhs3(grams[j])) for j in range(4)]
        traces = [half_sums(jnp.sum(lefts[j] * delta, axis=0, keepdims=True)) + EPS_TRACE for j in range(4)]
        scales = [1.0 / jnp.sqrt(traces[j]) for j in range(4)]
        normals = [dot(lhs3(lefts[j]), delta_r) for j in range(4)]
        curs, brackets = [], []
        for j in range(4):
            left_s[j] = lefts[j]
            curs.append(normals[j] * (1.0 / traces[j]))
            brackets.append(1.5 * eye - 0.5 * curs[j])
        firsts = [mm(brackets[j], curs[j]) for j in range(4)]
        for j in range(4):
            cr[j, :, 0:128] = firsts[j]
            cr[j, :, 128:256] = brackets[j]

        if it == 0:
            lax.fori_loop(0, 3, polar, 0)
            gather_sums(0)
            lax.fori_loop(0, POLAR - 5, polar, 0)
        elif it == 1:
            lax.fori_loop(0, POLAR - 2, polar, 0)
        else:
            lax.fori_loop(0, POLAR - 2, polar, 0)
        boths = [cr[j] for j in range(4)]
        prods = [mm(boths[j][:, 128:256], boths[j][:, 0:128]) for j in range(4)]
        roots = [mm(1.5 * eye - 0.5 * prods[j], boths[j][:, 128:256]) for j in range(4)]
        parts = [mm(roots[j], left_s[j]) * scales[j] for j in range(4)]
        for j in range(4):
            x_s[j] = roots[j]
        part = (parts[0] + parts[1]) + (parts[2] + parts[3])
        part = part + swap(part)
        packed = jnp.where(low, part[0:32], part[32:64])
        for q in range(4):
            qsend[it * 4 + q] = packed[8 * q : 8 * q + 8]
        for d in range(1, 4):
            to = lax.rem(quad + d, 4)
            send(qsend.at[it * 4 + to], qrecv.at[it, quad], q1_s, q1_r.at[it], quad_dev(to))
        qrecv[it, quad] = qsend[it * 4 + quad]
        if it == 1:
            smooth(1)
        delta_tl = lhs3(delta_t)
        for j in range(4):
            root = x_s[j]
            k_l[j] = lhs3(dot(delta_tl, rhs3(root)) * scales[j])
            if not last:
                gram_l[j] = lhs3(grams[j])
        arrived(qrecv.at[it, pl.ds(0, 3)], q1_s, q1_r.at[it])
        zbuf[it * 8 + zz] = (qrecv[it, 0] + qrecv[it, 1]) + (qrecv[it, 2] + qrecv[it, 3])
        for d in (4, 3, 5, 2, 6, 1, 7):
            slot = zbuf.at[it * 8 + zz]
            send(slot, slot, z_s, z_r.at[it], z_dev(lax.rem(zz + d, 8)))
        if last:
            for j in range(4):
                evo, tall = rows_of(j)
                talls[j] = tall
                evo_o[j] = evo[:, 0:64]
                evo_o[j + 4] = evo[:, 64:128]
        if it == 1:
            gather_sums(1)
        arrived(zbuf.at[pl.ds(it * 8, 7)], z_s, z_r.at[it])
        total = zbuf[it * 8]
        for z in range(1, 8):
            total = total + zbuf[it * 8 + z]
        qall[it * 4 + quad] = total * (1.0 / 256.0)
        for d in range(1, 4):
            slot = qall.at[it * 4 + quad]
            send(slot, slot, q2_s, q2_r.at[it], quad_dev(lax.rem(quad + d, 4)))
        if not last:
            from_chan(sall.at[it], s2_s, s2_r.at[it])
            for j in range(4):
                gut = jnp.concatenate([sall[it, 2 * j, 1], sall[it, 2 * j + 1, 1]], axis=0)
                gtu_s[j] = narrow(jnp.concatenate([gut, gut], axis=0).T)
        arrived(qall.at[pl.ds(it * 4, 3)], q2_s, q2_r.at[it])
        delta = unpack(jnp.concatenate([qall[it * 4 + q] for q in range(4)], axis=0))
        fresh_r = rhs3(delta)

        if last:
            mixers = [dot(k_l[j], fresh_r) for j in range(4)]
            coups = [mm(talls[j], mixers[j]) for j in range(4)]
            for j in range(4):
                coup_o[j] = coups[j][:, 0:64]
                coup_o[j + 4] = coups[j][:, 64:128]
            delta_o[...] = delta[:, 0:64]
        else:
            mixers = [dot(k_l[j], fresh_r) for j in range(4)]
            turns = [dot(lhs3(2.0 * mixers[j] - eye), x_rhs[j]) for j in range(4)]
            for j in range(4):
                mix_s[j, :, 0:128] = rhs3(turns[j])
                mix_s[j, :, 128:256] = rhs3(mixers[j])
            steps = [turns[j] + (eye - mixers[j]) for j in range(4)]
            sides = [gtu_s[j] + 0.5 * dot(gram_l[j], rhs3(steps[j])) for j in range(4)]
            delta_t = transposed(delta)
            if it == 0:
                fresh = [rows_of(j) for j in range(4)]
                for j in range(4):
                    evos[j], talls[j] = fresh[j]
                    at_s[1, j] = (fresh[j][0] + dss[j]) * a_rows[j : j + 1]
            grams = []
            for j in range(4):
                guu = jnp.concatenate([sall[it, 2 * j, 0], sall[it, 2 * j + 1, 0]], axis=0)
                grams.append(guu + narrow(gram_of([steps[j], sides[j]], [sides[j], steps[j]])))
            if it == 0:
                halo_send(at_s.at[1], hal_t.at[1], ht_s, ht_r.at[1])

    for ref, ssem, rsem in (
        (psend.at[pl.ds(0, 3)], px_s, px_r.at[0]),
        (ysend, py_s, py_r.at[0]),
        (fg.at[pl.ds(0, 7)], fg_s, fg_r),
        (gsend.at[pl.ds(0, 7)], g1_s, g1_r),
        (gall.at[pl.ds(0, 7)], g2_s, g2_r),
        (ssend.at[:, pl.ds(0, 7)], s1_s, s1_r.at[0]),
        (sall.at[:, pl.ds(0, 7)], s2_s, s2_r.at[0]),
        (qsend.at[pl.ds(0, 9)], q1_s, q1_r.at[0]),
        (zbuf.at[pl.ds(0, 21)], z_s, z_r.at[0]),
        (qall.at[pl.ds(0, 9)], q2_s, q2_r.at[0]),
        (hal_a, ha_s, ha_r.at[0]),
        (hal_t, ht_s, ht_r.at[0]),
        (hal_b, hb_s, hb_r),
    ):
        whole(ref, ssem, rsem).wait_send()


def body(data, order, chan_factor, slice_weights, smooth_aux, coupled, smooth_dual, coupling_dual, delta):
    vm = pltpu.VMEM
    dma = pltpu.SemaphoreType.DMA
    rows = (4, 48, 128)
    anyspace = pl.BlockSpec(memory_space=pl.ANY)
    vspace = pl.BlockSpec(memory_space=pltpu.VMEM)
    return pl.pallas_call(
        kernel,
        out_shape=(
            jax.ShapeDtypeStruct((8, 48, 64), F32),
            jax.ShapeDtypeStruct((8, 48, 64), F32),
            jax.ShapeDtypeStruct((64, 64), F32),
        ),
        in_specs=[pl.BlockSpec(memory_space=pltpu.SMEM)] + [anyspace] * 8,
        out_specs=(vspace, vspace, vspace),
        scratch_shapes=[
            vm((8, 384, 128), BF16), vm((64, 128), BF16), vm((8, 64), F32), vm((4, 8, 48, 64), F32), vm((64, 64), F32),
            vm((4, 4, 2, 48, 128), F32), vm((4, 4, 2, 48, 128), F32), vm(rows, F32), vm(rows, F32),
            vm((8, 32, 128), F32), vm((4, 64, 128), F32), vm((4, 64, 384), BF16), vm((4, 384, 128), BF16),
            vm((4, 64, 256), F32), vm((4, 64, 128), F32), vm((4, 64, 384), BF16),
            vm((4, 64, 384), BF16), vm((4, 64, 128), F32),
            vm((8, 32, 128), F32), vm((8, 32, 128), F32), vm((8, 32, 128), F32),
            vm((2, 8, 2, 32, 128), F32), vm((2, 8, 2, 32, 128), F32), vm((2, 8, 2, 32, 128), F32),
            vm((12, 8, 128), F32), vm((3, 4, 8, 128), F32), vm((24, 8, 128), F32), vm((12, 8, 128), F32),
            vm((2,) + rows, F32), vm(rows, F32), vm(rows, F32), vm(rows, F32), vm(rows, F32), vm((4, 384, 256), BF16),
            vm((2,) + rows, F32), vm(rows, F32),
            vm((2, 2) + rows, F32), vm((2, 2) + rows, F32), vm((8, 128), F32), vm((2, 8, 128), F32),
            dma((5,)), dma, dma((4,)), dma, dma((4,)), dma, dma, dma, dma, dma, dma, dma, dma((2,)), dma, dma((2,)),
            dma, dma((3,)), dma, dma((3,)), dma, dma((3,)), dma, dma((2,)), dma, dma((2,)), dma, dma,
        ],
        compiler_params=pltpu.CompilerParams(
            collective_id=0, has_side_effects=True, vmem_limit_bytes=60 * 1024 * 1024
        ),
    )(order, data, chan_factor.T, slice_weights, smooth_aux, coupled, smooth_dual, coupling_dual, delta)


def solution(mesh):
    return jax.shard_map(
        body,
        mesh=mesh,
        in_specs=(
            P("cuts", None, "chan"),
            P("cuts"),
            P("chan", None),
            P("cuts", None),
            P("cuts", "chan", None),
            P("cuts", "chan", None),
            P("cuts", "chan", None),
            P("cuts", "chan", None),
            P(),
        ),
        out_specs=(P("cuts", "chan", None), P("cuts", "chan", None), P()),
        check_vma=False,
    )
```

```python
import jax
import jax.numpy as jnp
from jax import lax
from jax.experimental import pallas as pl
from jax.experimental.pallas import tpu as pltpu
from jax.sharding import PartitionSpec as P

INNER = 3
POLAR = 8
NEWTON = 7
EPS_TRACE = 1e-06
F32 = jnp.float32
MESH = pl.DeviceIdType.MESH
CHEB_A = 0.1328125 / 1.2578125
CHEB_B = -1.0 / (512.0 * 1.2578125)


BF16 = jnp.bfloat16


def split(a):
    high = a.astype(BF16)
    return high, (a - high.astype(F32)).astype(BF16)


def lhs3(a):
    high, rest = split(a)
    return jnp.concatenate([high, rest, high], axis=1)


def dot(a, b):
    return jnp.dot(a, b, preferred_element_type=F32)


def gram_of(a, b):
    left, right = [], []
    for p, q in zip(a, b):
        ph, pl_ = split(p)
        qh, ql = split(q)
        left += [ph, pl_, ph]
        right += [qh, qh, ql]
    return lax.dot_general(
        jnp.concatenate(left, axis=0), jnp.concatenate(right, axis=0), (((0,), (0,)), ((), ())),
        preferred_element_type=F32,
    )


def kernel(
    order, data_h, fac_h, w_h, aux_h, coup_h, ds_h, dc_h, delta_h,
    out_o, delta_o,
    data_v, fac_v, w_v, rows_v, delta_v,
    psend, precv, ysend, yrecv, fg, x_s, sys_s, x_rhs, cr, left_s, k_l, gram_l, gtu_s,
    gsend, grecv, gall, ssend, srecv, sall, qsend, qrecv, zbuf, qall,
    aux_p, dss, talls, evos, us, mix_s, at_s, baux, hal_a, hal_t, bsend, hal_b,
    load_sem, px_s, px_r, py_s, py_r, fg_s, fg_r, g1_s, g1_r, g2_s, g2_r, s1_s, s1_r, s2_s, s2_r,
    q1_s, q1_r, z_s, z_r, q2_s, q2_r, ha_s, ha_r, ht_s, ht_r, hb_s, hb_r,
):
    cuts = lax.axis_index("cuts")
    chan = lax.axis_index("chan")
    core = lax.rem(cuts, 2)
    zz = lax.rem(cuts // 2, 8)
    ylo = cuts // 16
    quad = ylo * 2 + core
    xx = lax.rem(chan, 4)
    yhi = chan // 4
    left_id = lax.rem(cuts + 31, 32)
    right_id = lax.rem(cuts + 1, 32)

    def z_dev(z):
        return (ylo * 16 + z * 2 + core, chan)

    def quad_dev(q):
        return ((q // 2) * 16 + zz * 2 + lax.rem(q, 2), chan)

    def send(src, dst, ssem, rsem, dev):
        pltpu.make_async_remote_copy(
            src_ref=src, dst_ref=dst, send_sem=ssem, recv_sem=rsem, device_id=dev, device_id_type=MESH
        ).start()

    def whole(ref, ssem, rsem):
        return pltpu.make_async_remote_copy(
            src_ref=ref, dst_ref=ref, send_sem=ssem, recv_sem=rsem, device_id=(left_id, chan), device_id_type=MESH
        )

    def arrived(ref, ssem, rsem):
        whole(ref, ssem, rsem).wait_recv()

    def load(src, dst, n):
        return pltpu.make_async_copy(src, dst, load_sem.at[n])

    load(fac_h, fac_v, 0).start()
    load(data_h, data_v, 1).start()
    load(w_h, w_v, 2).start()
    for n, src in enumerate((aux_h, coup_h, ds_h, dc_h)):
        load(src, rows_v.at[n], 3).start()
    load(delta_h, delta_v, 4).start()

    barrier = pltpu.get_barrier_semaphore()
    greet = [(cuts, lax.rem(chan + d, 8)) for d in range(1, 8)]
    greet += [z_dev(lax.rem(zz + d, 8)) for d in range(1, 8)]
    greet += [quad_dev(lax.rem(quad + d, 4)) for d in range(1, 4)]
    greet += [(left_id, chan), (right_id, chan)]
    for dev in greet:
        pl.semaphore_signal(barrier, inc=1, device_id=dev, device_id_type=MESH)

    lane = lax.broadcasted_iota(jnp.int32, (1, 128), 1)
    low = lane < 64
    high = lane >= 64
    row_i = lax.broadcasted_iota(jnp.int32, (64, 128), 0)
    col_i = lax.broadcasted_iota(jnp.int32, (64, 128), 1)
    eye_b = row_i == lax.rem(col_i, 64)
    eye = eye_b.astype(F32)
    low16 = low.astype(F32).astype(BF16)
    high16 = high.astype(F32).astype(BF16)

    def swap(v):
        return pltpu.roll(v, 64, 1)

    def widen(v):
        return jnp.concatenate([v * low16, v * high16], axis=0)

    def rhs3(a):
        first, rest = split(a)
        first, rest = widen(first), widen(rest)
        return jnp.concatenate([first, first, rest], axis=0)

    def mm(a, b):
        return dot(lhs3(a), rhs3(b))

    def narrow(t):
        return jnp.where(low, t[0:64], t[64:128])

    def unpack(p):
        q = swap(p)
        return jnp.concatenate([jnp.where(low, p, q), jnp.where(low, q, p)], axis=0)

    def transposed(c):
        return jnp.concatenate([c, c], axis=0).T[0:64]

    def half_sums(v):
        zero = jnp.zeros_like(v)
        lo = jnp.sum(jnp.where(low, v, zero), axis=1, keepdims=True)
        hi = jnp.sum(jnp.where(low, zero, v), axis=1, keepdims=True)
        return jnp.where(low, lo, hi)

    load(fac_h, fac_v, 0).wait()
    fac = fac_v[...]
    nt = (((1,), (1,)), ((), ()))
    partial_gram = lax.dot_general(fac, fac, nt, preferred_element_type=F32)
    fg[chan] = jnp.concatenate([partial_gram[0:32], partial_gram[32:64]], axis=1)
    zero_fac = jnp.zeros_like(fac)
    fac2 = jnp.concatenate(
        [jnp.concatenate([fac, zero_fac], axis=1), jnp.concatenate([zero_fac, fac], axis=1)], axis=0
    )
    load(data_h, data_v, 1).wait()
    for j in range(4):
        first = data_v[lax.rem(order[j], 8)]
        second = data_v[lax.rem(order[j + 4], 8)]
        out = lax.dot_general(jnp.concatenate([first, second], axis=1), fac2, nt, preferred_element_type=F32)
        for c in range(8):
            psend[j, c % 4, c // 4] = out[48 * c : 48 * c + 48]
    pl.semaphore_wait(barrier, len(greet))
    for d in range(1, 8):
        peer = lax.rem(chan + d, 8)
        send(fg.at[chan], fg.at[chan], fg_s, fg_r, (cuts, peer))
    for j in range(4):
        for d in (2, 1, 3):
            to = lax.rem(xx + d, 4)
            send(psend.at[j, to], precv.at[j, xx], px_s, px_r.at[j], (cuts, yhi * 4 + to))

    load(w_h, w_v, 2).wait()
    load(rows_v, rows_v, 3).wait()
    load(delta_h, delta_v, 4).wait()

    def pair(n, j):
        return jnp.concatenate([rows_v[n, j], rows_v[n, j + 4]], axis=1)

    for j in range(4):
        aux_p[0, j] = pair(0, j)
        dss[j] = pair(2, j)
        dual = pair(3, j)
        talls[j] = dual
        us[j] = pair(1, j) - dual

    def halo_send(src, dst, ssem, rsem):
        send(src, dst.at[0], ssem, rsem, (right_id, chan))
        send(src, dst.at[1], ssem, rsem, (left_id, chan))

    halo_send(aux_p.at[0], hal_a.at[0], ha_s, ha_r.at[0])

    arrived(fg.at[pl.ds(0, 7)], fg_s, fg_r)
    gram_sum = fg[0]
    for c in range(1, 8):
        gram_sum = gram_sum + fg[c]
    gram2 = unpack(gram_sum)
    w = w_v[...]
    w2 = jnp.concatenate([w[0:4], w[4:8]], axis=1)
    diag_row = jnp.sum(jnp.where(eye_b, gram2, 0.0), axis=0, keepdims=True)
    rho = half_sums(w2 * w2 * diag_row) * (1.0 / 64.0)
    w_over = w2 / rho
    b_rows = 2.0 / (rho + 4.0)
    a_rows = rho / (rho + 4.0)
    bsend[0:4] = b_rows
    bsend[4:8] = b_rows
    halo_send(bsend, hal_b, hb_s, hb_r)
    for j in range(4):
        w_col = half_sums(jnp.where(eye_b, w2[j : j + 1], 0.0))
        system = gram2 * w_col * w_over[j : j + 1] + 2.0 * eye
        sys_s[j] = lhs3(system)
        x_s[j] = CHEB_A * eye + CHEB_B * system

    def newton(step, carry):
        xs = [x_s[j] for j in range(4)]
        gaps = [2.0 * eye - dot(sys_s[j], rhs3(xs[j])) for j in range(4)]
        fresh = [mm(xs[j], gaps[j]) for j in range(4)]
        for j in range(4):
            x_s[j] = fresh[j]
        return carry

    def forward(j):
        arrived(precv.at[j, pl.ds(0, 3)], px_s, px_r.at[j])
        total = psend[j, xx, 1 - yhi]
        for d in range(1, 4):
            total = total + precv[j, lax.rem(xx + d, 4), 1 - yhi]
        ysend[j] = total
        send(ysend.at[j], yrecv.at[j], py_s, py_r.at[j], (cuts, (1 - yhi) * 4 + xx))
        total = psend[j, xx, yhi]
        for d in range(1, 4):
            total = total + precv[j, lax.rem(xx + d, 4), yhi]
        baux[j] = total

    lax.fori_loop(0, 2, newton, 0)
    forward(0)
    lax.fori_loop(0, 3, newton, 0)
    forward(1)
    lax.fori_loop(0, NEWTON - 5, newton, 0)
    forward(2)
    for j in range(4):
        x_rhs[j] = rhs3(x_s[j])
    forward(3)

    delta_in = delta_v[...]
    delta = jnp.concatenate([delta_in, delta_in], axis=1)

    def spread(buf, ssem, rsem, own):
        buf[chan] = own
        for d in range(1, 8):
            send(buf.at[chan], buf.at[chan], ssem, rsem, (cuts, lax.rem(chan + d, 8)))

    def scatter(src, dst, ssem, rsem):
        for d in range(1, 8):
            peer = lax.rem(chan + d, 8)
            send(src.at[peer], dst.at[chan], ssem, rsem, (cuts, peer))
        dst[chan] = src[chan]

    def from_chan(buf, ssem, rsem):
        arrived(buf.at[pl.ds(0, 7)], ssem, rsem)

    def total_of(buf):
        total = buf[0]
        for c in range(1, 8):
            total = total + buf[c]
        return total

    def smooth(it):
        arrived(hal_a.at[it], ha_s, ha_r.at[it])
        arrived(hal_t.at[it], ht_s, ht_r.at[it])
        if it == 0:
            arrived(hal_b, hb_s, hb_r)
        vals, tars, bs = [], [], []
        for p in range(4):
            vals.append(jnp.where(low, swap(hal_a[it, 0, p]), aux_p[it, p]))
            tars.append(jnp.where(low, swap(hal_t[it, 0, p]), at_s[it, p]))
            bs.append(jnp.where(low, swap(hal_b[0, p : p + 1]), bsend[p : p + 1]))
        for p in range(4):
            vals.append(jnp.where(low, aux_p[it, p], swap(hal_a[it, 1, p])))
            tars.append(jnp.where(low, at_s[it, p], swap(hal_t[it, 1, p])))
            bs.append(jnp.where(low, bsend[p : p + 1], swap(hal_b[1, p : p + 1])))
        for sweep in range(4):
            fresh = []
            for p in range(8):
                before = vals[p - 1] if p > 0 else swap(vals[7])
                after = vals[p + 1] if p < 7 else swap(vals[0])
                fresh.append(tars[p] + bs[p] * (before + after))
            vals = fresh
        for j in range(4):
            aux = jnp.where(low, vals[4 + j], vals[j])
            dual = dss[j] + evos[j] - aux
            if it == 0:
                aux_p[1, j] = aux
            dss[j] = dual
            us[j] = dot(lhs3(baux[j] + (aux - dual)), x_rhs[j])
        if it == 0:
            halo_send(aux_p.at[1], hal_a.at[1], ha_s, ha_r.at[1])
        for j in range(4):
            u, tall = us[j], talls[j]
            sums = gram_of([u], [jnp.concatenate([u, tall], axis=1)])
            guu, gut = narrow(sums[:, 0:128]), narrow(sums[:, 128:256])
            for h in range(2):
                ssend[it, 2 * j + h, 0] = guu[32 * h : 32 * h + 32]
                ssend[it, 2 * j + h, 1] = gut[32 * h : 32 * h + 32]
        scatter(ssend.at[it], srecv.at[it], s1_s, s1_r.at[it])

    def gather_sums(it):
        from_chan(srecv.at[it], s1_s, s1_r.at[it])
        spread(sall.at[it], s2_s, s2_r.at[it], total_of(srecv.at[it]))

    def rows_of(j):
        tall = talls[j]
        both = dot(lhs3(tall), mix_s[j])
        evo = us[j] + both[:, 0:128]
        return evo, evo + (tall - both[:, 128:256])

    def polar(step, carry):
        for j in range(4):
            both = cr[j]
            root = both[:, 128:256]
            ch, cl = split(both[:, 0:128])
            rh, rl = split(root)
            ch, cl = widen(ch), widen(cl)
            prod = dot(lhs3(root), jnp.concatenate([ch, ch, cl], axis=0))
            firsts = jnp.concatenate([ch, widen(rh)], axis=1)
            rests = jnp.concatenate([cl, widen(rl)], axis=1)
            bracket = 1.5 * eye - 0.5 * prod
            cr[j] = dot(lhs3(bracket), jnp.concatenate([firsts, firsts, rests], axis=0))
        return carry

    fresh = []
    for j in range(4):
        arrived(yrecv.at[j], py_s, py_r.at[j])
        baux[j] = (baux[j] + yrecv[j]) * w_over[j : j + 1]
        fresh.append(dot(lhs3(baux[j] + (aux_p[0, j] - dss[j]) + us[j]), x_rhs[j]))
    for j in range(4):
        tall = fresh[j] + talls[j]
        evos[j] = fresh[j]
        talls[j] = tall
        part = narrow(gram_of([tall], [tall]))
        gsend[2 * j] = part[0:32]
        gsend[2 * j + 1] = part[32:64]
    scatter(gsend, grecv, g1_s, g1_r)
    for j in range(4):
        at_s[0, j] = (evos[j] + dss[j]) * a_rows[j : j + 1]
    halo_send(at_s.at[0], hal_t.at[0], ht_s, ht_r.at[0])
    from_chan(grecv, g1_s, g1_r)
    spread(gall, g2_s, g2_r, total_of(grecv))
    smooth(0)
    delta_t = transposed(delta)
    from_chan(gall, g2_s, g2_r)
    grams = [jnp.concatenate([gall[2 * j], gall[2 * j + 1]], axis=0) for j in range(4)]

    for it in range(INNER):
        last = it == INNER - 1
        delta_l = lhs3(delta)
        delta_r = rhs3(delta_t)
        lefts = [dot(delta_l, rhs3(grams[j])) for j in range(4)]
        traces = [half_sums(jnp.sum(lefts[j] * delta, axis=0, keepdims=True)) + EPS_TRACE for j in range(4)]
        scales = [1.0 / jnp.sqrt(traces[j]) for j in range(4)]
        normals = [dot(lhs3(lefts[j]), delta_r) for j in range(4)]
        curs, brackets = [], []
        for j in range(4):
            left_s[j] = lefts[j]
            curs.append(normals[j] * (1.0 / traces[j]))
            brackets.append(1.5 * eye - 0.5 * curs[j])
        firsts = [mm(brackets[j], curs[j]) for j in range(4)]
        for j in range(4):
            cr[j, :, 0:128] = firsts[j]
            cr[j, :, 128:256] = brackets[j]

        if it == 0:
            lax.fori_loop(0, 3, polar, 0)
            gather_sums(0)
            lax.fori_loop(0, POLAR - 5, polar, 0)
        elif it == 1:
            lax.fori_loop(0, 2, polar, 0)
            smooth(1)
            lax.fori_loop(0, POLAR - 4, polar, 0)
        else:
            lax.fori_loop(0, POLAR - 2, polar, 0)
        boths = [cr[j] for j in range(4)]
        prods = [mm(boths[j][:, 128:256], boths[j][:, 0:128]) for j in range(4)]
        roots = [mm(1.5 * eye - 0.5 * prods[j], boths[j][:, 128:256]) for j in range(4)]
        parts = [mm(roots[j], left_s[j]) * scales[j] for j in range(4)]
        for j in range(4):
            x_s[j] = roots[j]
        part = (parts[0] + parts[1]) + (parts[2] + parts[3])
        part = part + swap(part)
        packed = jnp.where(low, part[0:32], part[32:64])
        for q in range(4):
            qsend[it * 4 + q] = packed[8 * q : 8 * q + 8]
        for d in range(1, 4):
            to = lax.rem(quad + d, 4)
            send(qsend.at[it * 4 + to], qrecv.at[it, quad], q1_s, q1_r.at[it], quad_dev(to))
        qrecv[it, quad] = qsend[it * 4 + quad]
        if it == 1:
            gather_sums(1)
        delta_tl = lhs3(delta_t)
        for j in range(4):
            root = x_s[j]
            k_l[j] = lhs3(dot(delta_tl, rhs3(root)) * scales[j])
            if not last:
                gram_l[j] = lhs3(grams[j])
        arrived(qrecv.at[it, pl.ds(0, 3)], q1_s, q1_r.at[it])
        zbuf[it * 8 + zz] = (qrecv[it, 0] + qrecv[it, 1]) + (qrecv[it, 2] + qrecv[it, 3])
        for d in (4, 3, 5, 2, 6, 1, 7):
            slot = zbuf.at[it * 8 + zz]
            send(slot, slot, z_s, z_r.at[it], z_dev(lax.rem(zz + d, 8)))
        if last:
            for j in range(4):
                evo, tall = rows_of(j)
                talls[j] = tall
                out_o[j] = evo
        arrived(zbuf.at[pl.ds(it * 8, 7)], z_s, z_r.at[it])
        total = zbuf[it * 8]
        for z in range(1, 8):
            total = total + zbuf[it * 8 + z]
        qall[it * 4 + quad] = total * (1.0 / 256.0)
        for d in range(1, 4):
            slot = qall.at[it * 4 + quad]
            send(slot, slot, q2_s, q2_r.at[it], quad_dev(lax.rem(quad + d, 4)))
        if not last:
            from_chan(sall.at[it], s2_s, s2_r.at[it])
            for j in range(4):
                gut = jnp.concatenate([sall[it, 2 * j, 1], sall[it, 2 * j + 1, 1]], axis=0)
                gtu_s[j] = narrow(jnp.concatenate([gut, gut], axis=0).T)
        arrived(qall.at[pl.ds(it * 4, 3)], q2_s, q2_r.at[it])
        delta = unpack(jnp.concatenate([qall[it * 4 + q] for q in range(4)], axis=0))
        fresh_r = rhs3(delta)

        if last:
            mixers = [dot(k_l[j], fresh_r) for j in range(4)]
            coups = [mm(talls[j], mixers[j]) for j in range(4)]
            for j in range(4):
                out_o[4 + j] = coups[j]
            delta_o[...] = delta[:, 0:64]
        else:
            mixers = [dot(k_l[j], fresh_r) for j in range(4)]
            turns = [dot(lhs3(2.0 * mixers[j] - eye), x_rhs[j]) for j in range(4)]
            for j in range(4):
                mix_s[j, :, 0:128] = rhs3(turns[j])
                mix_s[j, :, 128:256] = rhs3(mixers[j])
            steps = [turns[j] + (eye - mixers[j]) for j in range(4)]
            sides = [gtu_s[j] + 0.5 * dot(gram_l[j], rhs3(steps[j])) for j in range(4)]
            delta_t = transposed(delta)
            if it == 0:
                fresh = [rows_of(j) for j in range(4)]
                for j in range(4):
                    evos[j], talls[j] = fresh[j]
                    at_s[1, j] = (fresh[j][0] + dss[j]) * a_rows[j : j + 1]
            grams = []
            for j in range(4):
                guu = jnp.concatenate([sall[it, 2 * j, 0], sall[it, 2 * j + 1, 0]], axis=0)
                grams.append(guu + narrow(gram_of([steps[j], sides[j]], [sides[j], steps[j]])))
            if it == 0:
                halo_send(at_s.at[1], hal_t.at[1], ht_s, ht_r.at[1])

    for ref, ssem, rsem in (
        (psend.at[pl.ds(0, 3)], px_s, px_r.at[0]),
        (ysend, py_s, py_r.at[0]),
        (fg.at[pl.ds(0, 7)], fg_s, fg_r),
        (gsend.at[pl.ds(0, 7)], g1_s, g1_r),
        (gall.at[pl.ds(0, 7)], g2_s, g2_r),
        (ssend.at[:, pl.ds(0, 7)], s1_s, s1_r.at[0]),
        (sall.at[:, pl.ds(0, 7)], s2_s, s2_r.at[0]),
        (qsend.at[pl.ds(0, 9)], q1_s, q1_r.at[0]),
        (zbuf.at[pl.ds(0, 21)], z_s, z_r.at[0]),
        (qall.at[pl.ds(0, 9)], q2_s, q2_r.at[0]),
        (hal_a, ha_s, ha_r.at[0]),
        (hal_t, ht_s, ht_r.at[0]),
        (hal_b, hb_s, hb_r),
    ):
        whole(ref, ssem, rsem).wait_send()


def unpair(out_p, delta_p, evo_o, coup_o, delta_o):
    for j in range(4):
        evo, coup = out_p[j], out_p[4 + j]
        evo_o[j] = evo[:, 0:64]
        evo_o[j + 4] = evo[:, 64:128]
        coup_o[j] = coup[:, 0:64]
        coup_o[j + 4] = coup[:, 64:128]
    delta_o[...] = delta_p[...]


def body(data, order, chan_factor, slice_weights, smooth_aux, coupled, smooth_dual, coupling_dual, delta):
    vm = pltpu.VMEM
    dma = pltpu.SemaphoreType.DMA
    rows = (4, 48, 128)
    anyspace = pl.BlockSpec(memory_space=pl.ANY)
    vspace = pl.BlockSpec(memory_space=pltpu.VMEM)
    paired, delta_out = pl.pallas_call(
        kernel,
        out_shape=(jax.ShapeDtypeStruct((8, 48, 128), F32), jax.ShapeDtypeStruct((64, 64), F32)),
        in_specs=[pl.BlockSpec(memory_space=pltpu.SMEM)] + [anyspace] * 8,
        out_specs=(vspace, vspace),
        scratch_shapes=[
            vm((8, 384, 128), BF16), vm((64, 128), BF16), vm((8, 64), F32), vm((4, 8, 48, 64), F32), vm((64, 64), F32),
            vm((4, 4, 2, 48, 128), F32), vm((4, 4, 2, 48, 128), F32), vm(rows, F32), vm(rows, F32),
            vm((8, 32, 128), F32), vm((4, 64, 128), F32), vm((4, 64, 384), BF16), vm((4, 384, 128), BF16),
            vm((4, 64, 256), F32), vm((4, 64, 128), F32), vm((4, 64, 384), BF16),
            vm((4, 64, 384), BF16), vm((4, 64, 128), F32),
            vm((8, 32, 128), F32), vm((8, 32, 128), F32), vm((8, 32, 128), F32),
            vm((2, 8, 2, 32, 128), F32), vm((2, 8, 2, 32, 128), F32), vm((2, 8, 2, 32, 128), F32),
            vm((12, 8, 128), F32), vm((3, 4, 8, 128), F32), vm((24, 8, 128), F32), vm((12, 8, 128), F32),
            vm((2,) + rows, F32), vm(rows, F32), vm(rows, F32), vm(rows, F32), vm(rows, F32), vm((4, 384, 256), BF16),
            vm((2,) + rows, F32), vm(rows, F32),
            vm((2, 2) + rows, F32), vm((2, 2) + rows, F32), vm((8, 128), F32), vm((2, 8, 128), F32),
            dma((5,)), dma, dma((4,)), dma, dma((4,)), dma, dma, dma, dma, dma, dma, dma, dma((2,)), dma, dma((2,)),
            dma, dma((3,)), dma, dma((3,)), dma, dma((3,)), dma, dma((2,)), dma, dma((2,)), dma, dma,
        ],
        compiler_params=pltpu.CompilerParams(
            collective_id=0, has_side_effects=True, vmem_limit_bytes=60 * 1024 * 1024
        ),
    )(order, data, chan_factor.T, slice_weights, smooth_aux, coupled, smooth_dual, coupling_dual, delta)
    return pl.pallas_call(
        unpair,
        out_shape=(
            jax.ShapeDtypeStruct((8, 48, 64), F32),
            jax.ShapeDtypeStruct((8, 48, 64), F32),
            jax.ShapeDtypeStruct((64, 64), F32),
        ),
        in_specs=[vspace, vspace],
        out_specs=(vspace, vspace, vspace),
    )(paired, delta_out)


def solution(mesh):
    return jax.shard_map(
        body,
        mesh=mesh,
        in_specs=(
            P("cuts", None, "chan"),
            P("cuts"),
            P("chan", None),
            P("cuts", None),
            P("cuts", "chan", None),
            P("cuts", "chan", None),
            P("cuts", "chan", None),
            P("cuts", "chan", None),
            P(),
        ),
        out_specs=(P("cuts", "chan", None), P("cuts", "chan", None), P()),
        check_vma=False,
    )
```

```python
import jax
import jax.numpy as jnp
from jax import lax
from jax.experimental import pallas as pl
from jax.experimental.pallas import tpu as pltpu
from jax.sharding import PartitionSpec as P

INNER = 3
POLAR = 8
NEWTON = 7
EPS_TRACE = 1e-06
F32 = jnp.float32
MESH = pl.DeviceIdType.MESH
CHEB_A = 0.1328125 / 1.2578125
CHEB_B = -1.0 / (512.0 * 1.2578125)


BF16 = jnp.bfloat16


def split(a):
    high = a.astype(BF16)
    return high, (a - high.astype(F32)).astype(BF16)


def lhs3(a):
    high, rest = split(a)
    return jnp.concatenate([high, rest, high], axis=1)


def dot(a, b):
    return jnp.dot(a, b, preferred_element_type=F32)


def gram_of(a, b):
    left, right = [], []
    for p, q in zip(a, b):
        ph, pl_ = split(p)
        qh, ql = split(q)
        left += [ph, pl_, ph]
        right += [qh, qh, ql]
    return lax.dot_general(
        jnp.concatenate(left, axis=0), jnp.concatenate(right, axis=0), (((0,), (0,)), ((), ())),
        preferred_element_type=F32,
    )


def kernel(
    order, data_h, fac_h, w_h, aux_h, coup_h, ds_h, dc_h, delta_h,
    out_o, delta_o,
    data_v, fac_v, w_v, rows_v, delta_v,
    psend, precv, ysend, yrecv, fg, x_s, sys_s, x_rhs, cr, left_s, k_l, gram_l, gtu_s,
    gsend, grecv, gall, ssend, srecv, sall, qsend, qrecv, zbuf,
    aux_p, dss, talls, evos, us, mix_s, at_s, baux, hal_a, hal_t, bsend, hal_b,
    load_sem, px_s, px_r, py_s, py_r, fg_s, fg_r, g1_s, g1_r, g2_s, g2_r, s1_s, s1_r, s2_s, s2_r,
    q1_s, q1_r, z_s, z_r, ha_s, ha_r, ht_s, ht_r, hb_s, hb_r,
):
    cuts = lax.axis_index("cuts")
    chan = lax.axis_index("chan")
    core = lax.rem(cuts, 2)
    zz = lax.rem(cuts // 2, 8)
    ylo = cuts // 16
    quad = ylo * 2 + core
    xx = lax.rem(chan, 4)
    yhi = chan // 4
    left_id = lax.rem(cuts + 31, 32)
    right_id = lax.rem(cuts + 1, 32)

    def z_dev(z):
        return (ylo * 16 + z * 2 + core, chan)

    def quad_dev(q):
        return ((q // 2) * 16 + zz * 2 + lax.rem(q, 2), chan)

    def send(src, dst, ssem, rsem, dev):
        pltpu.make_async_remote_copy(
            src_ref=src, dst_ref=dst, send_sem=ssem, recv_sem=rsem, device_id=dev, device_id_type=MESH
        ).start()

    def whole(ref, ssem, rsem):
        return pltpu.make_async_remote_copy(
            src_ref=ref, dst_ref=ref, send_sem=ssem, recv_sem=rsem, device_id=(left_id, chan), device_id_type=MESH
        )

    def arrived(ref, ssem, rsem):
        whole(ref, ssem, rsem).wait_recv()

    def load(src, dst, n):
        return pltpu.make_async_copy(src, dst, load_sem.at[n])

    load(fac_h, fac_v, 0).start()
    load(data_h, data_v, 1).start()
    load(w_h, w_v, 2).start()
    for n, src in enumerate((aux_h, coup_h, ds_h, dc_h)):
        load(src, rows_v.at[n], 3).start()
    load(delta_h, delta_v, 4).start()

    barrier = pltpu.get_barrier_semaphore()
    greet = [(cuts, lax.rem(chan + d, 8)) for d in range(1, 8)]
    greet += [(lax.rem(cuts + d, 32), chan) for d in range(1, 32)]
    for dev in greet:
        pl.semaphore_signal(barrier, inc=1, device_id=dev, device_id_type=MESH)

    lane = lax.broadcasted_iota(jnp.int32, (1, 128), 1)
    low = lane < 64
    high = lane >= 64
    row_i = lax.broadcasted_iota(jnp.int32, (64, 128), 0)
    col_i = lax.broadcasted_iota(jnp.int32, (64, 128), 1)
    eye_b = row_i == lax.rem(col_i, 64)
    eye = eye_b.astype(F32)
    low16 = low.astype(F32).astype(BF16)
    high16 = high.astype(F32).astype(BF16)

    def swap(v):
        return pltpu.roll(v, 64, 1)

    def widen(v):
        return jnp.concatenate([v * low16, v * high16], axis=0)

    def rhs3(a):
        first, rest = split(a)
        first, rest = widen(first), widen(rest)
        return jnp.concatenate([first, first, rest], axis=0)

    def mm(a, b):
        return dot(lhs3(a), rhs3(b))

    def narrow(t):
        return jnp.where(low, t[0:64], t[64:128])

    def unpack(p):
        q = swap(p)
        return jnp.concatenate([jnp.where(low, p, q), jnp.where(low, q, p)], axis=0)

    def transposed(c):
        return jnp.concatenate([c, c], axis=0).T[0:64]

    def half_sums(v):
        zero = jnp.zeros_like(v)
        lo = jnp.sum(jnp.where(low, v, zero), axis=1, keepdims=True)
        hi = jnp.sum(jnp.where(low, zero, v), axis=1, keepdims=True)
        return jnp.where(low, lo, hi)

    load(fac_h, fac_v, 0).wait()
    fac = fac_v[...]
    nt = (((1,), (1,)), ((), ()))
    partial_gram = lax.dot_general(fac, fac, nt, preferred_element_type=F32)
    fg[chan] = jnp.concatenate([partial_gram[0:32], partial_gram[32:64]], axis=1)
    zero_fac = jnp.zeros_like(fac)
    fac2 = jnp.concatenate(
        [jnp.concatenate([fac, zero_fac], axis=1), jnp.concatenate([zero_fac, fac], axis=1)], axis=0
    )
    load(data_h, data_v, 1).wait()
    for j in range(4):
        first = data_v[lax.rem(order[j], 8)]
        second = data_v[lax.rem(order[j + 4], 8)]
        out = lax.dot_general(jnp.concatenate([first, second], axis=1), fac2, nt, preferred_element_type=F32)
        for c in range(8):
            psend[j, c % 4, c // 4] = out[48 * c : 48 * c + 48]
    pl.semaphore_wait(barrier, len(greet))
    for d in range(1, 8):
        peer = lax.rem(chan + d, 8)
        send(fg.at[chan], fg.at[chan], fg_s, fg_r, (cuts, peer))
    for j in range(4):
        for d in (2, 1, 3):
            to = lax.rem(xx + d, 4)
            send(psend.at[j, to], precv.at[j, xx], px_s, px_r.at[j], (cuts, yhi * 4 + to))

    load(w_h, w_v, 2).wait()
    load(rows_v, rows_v, 3).wait()
    load(delta_h, delta_v, 4).wait()

    def pair(n, j):
        return jnp.concatenate([rows_v[n, j], rows_v[n, j + 4]], axis=1)

    for j in range(4):
        aux_p[0, j] = pair(0, j)
        dss[j] = pair(2, j)
        dual = pair(3, j)
        talls[j] = dual
        us[j] = pair(1, j) - dual

    def halo_send(src, dst, ssem, rsem):
        send(src, dst.at[0], ssem, rsem, (right_id, chan))
        send(src, dst.at[1], ssem, rsem, (left_id, chan))

    halo_send(aux_p.at[0], hal_a.at[0], ha_s, ha_r.at[0])

    arrived(fg.at[pl.ds(0, 7)], fg_s, fg_r)
    gram_sum = fg[0]
    for c in range(1, 8):
        gram_sum = gram_sum + fg[c]
    gram2 = unpack(gram_sum)
    w = w_v[...]
    w2 = jnp.concatenate([w[0:4], w[4:8]], axis=1)
    diag_row = jnp.sum(jnp.where(eye_b, gram2, 0.0), axis=0, keepdims=True)
    rho = half_sums(w2 * w2 * diag_row) * (1.0 / 64.0)
    w_over = w2 / rho
    b_rows = 2.0 / (rho + 4.0)
    a_rows = rho / (rho + 4.0)
    bsend[0:4] = b_rows
    bsend[4:8] = b_rows
    halo_send(bsend, hal_b, hb_s, hb_r)
    for j in range(4):
        w_col = half_sums(jnp.where(eye_b, w2[j : j + 1], 0.0))
        system = gram2 * w_col * w_over[j : j + 1] + 2.0 * eye
        sys_s[j] = lhs3(system)
        x_s[j] = CHEB_A * eye + CHEB_B * system

    def newton(step, carry):
        xs = [x_s[j] for j in range(4)]
        gaps = [2.0 * eye - dot(sys_s[j], rhs3(xs[j])) for j in range(4)]
        fresh = [mm(xs[j], gaps[j]) for j in range(4)]
        for j in range(4):
            x_s[j] = fresh[j]
        return carry

    def forward(j):
        arrived(precv.at[j, pl.ds(0, 3)], px_s, px_r.at[j])
        total = psend[j, xx, 1 - yhi]
        for d in range(1, 4):
            total = total + precv[j, lax.rem(xx + d, 4), 1 - yhi]
        ysend[j] = total
        send(ysend.at[j], yrecv.at[j], py_s, py_r.at[j], (cuts, (1 - yhi) * 4 + xx))
        total = psend[j, xx, yhi]
        for d in range(1, 4):
            total = total + precv[j, lax.rem(xx + d, 4), yhi]
        baux[j] = total

    lax.fori_loop(0, 2, newton, 0)
    forward(0)
    lax.fori_loop(0, 3, newton, 0)
    forward(1)
    lax.fori_loop(0, NEWTON - 5, newton, 0)
    forward(2)
    for j in range(4):
        x_rhs[j] = rhs3(x_s[j])
    forward(3)

    delta_in = delta_v[...]
    delta = jnp.concatenate([delta_in, delta_in], axis=1)

    def spread(buf, ssem, rsem, own):
        buf[chan] = own
        for d in range(1, 8):
            send(buf.at[chan], buf.at[chan], ssem, rsem, (cuts, lax.rem(chan + d, 8)))

    def scatter(src, dst, ssem, rsem):
        for d in range(1, 8):
            peer = lax.rem(chan + d, 8)
            send(src.at[peer], dst.at[chan], ssem, rsem, (cuts, peer))
        dst[chan] = src[chan]

    def from_chan(buf, ssem, rsem):
        arrived(buf.at[pl.ds(0, 7)], ssem, rsem)

    def total_of(buf):
        total = buf[0]
        for c in range(1, 8):
            total = total + buf[c]
        return total

    def smooth(it):
        arrived(hal_a.at[it], ha_s, ha_r.at[it])
        arrived(hal_t.at[it], ht_s, ht_r.at[it])
        if it == 0:
            arrived(hal_b, hb_s, hb_r)
        vals, tars, bs = [], [], []
        for p in range(4):
            vals.append(jnp.where(low, swap(hal_a[it, 0, p]), aux_p[it, p]))
            tars.append(jnp.where(low, swap(hal_t[it, 0, p]), at_s[it, p]))
            bs.append(jnp.where(low, swap(hal_b[0, p : p + 1]), bsend[p : p + 1]))
        for p in range(4):
            vals.append(jnp.where(low, aux_p[it, p], swap(hal_a[it, 1, p])))
            tars.append(jnp.where(low, at_s[it, p], swap(hal_t[it, 1, p])))
            bs.append(jnp.where(low, bsend[p : p + 1], swap(hal_b[1, p : p + 1])))
        for sweep in range(4):
            fresh = []
            for p in range(8):
                before = vals[p - 1] if p > 0 else swap(vals[7])
                after = vals[p + 1] if p < 7 else swap(vals[0])
                fresh.append(tars[p] + bs[p] * (before + after))
            vals = fresh
        for j in range(4):
            aux = jnp.where(low, vals[4 + j], vals[j])
            dual = dss[j] + evos[j] - aux
            if it == 0:
                aux_p[1, j] = aux
            dss[j] = dual
            us[j] = dot(lhs3(baux[j] + (aux - dual)), x_rhs[j])
        if it == 0:
            halo_send(aux_p.at[1], hal_a.at[1], ha_s, ha_r.at[1])
        for j in range(4):
            u, tall = us[j], talls[j]
            sums = gram_of([u], [jnp.concatenate([u, tall], axis=1)])
            guu, gut = narrow(sums[:, 0:128]), narrow(sums[:, 128:256])
            for h in range(2):
                ssend[it, 2 * j + h, 0] = guu[32 * h : 32 * h + 32]
                ssend[it, 2 * j + h, 1] = gut[32 * h : 32 * h + 32]
        scatter(ssend.at[it], srecv.at[it], s1_s, s1_r.at[it])

    def gather_sums(it):
        from_chan(srecv.at[it], s1_s, s1_r.at[it])
        spread(sall.at[it], s2_s, s2_r.at[it], total_of(srecv.at[it]))

    def rows_of(j):
        tall = talls[j]
        both = dot(lhs3(tall), mix_s[j])
        evo = us[j] + both[:, 0:128]
        return evo, evo + (tall - both[:, 128:256])

    def polar(step, carry):
        for j in range(4):
            both = cr[j]
            root = both[:, 128:256]
            ch, cl = split(both[:, 0:128])
            rh, rl = split(root)
            ch, cl = widen(ch), widen(cl)
            prod = dot(lhs3(root), jnp.concatenate([ch, ch, cl], axis=0))
            firsts = jnp.concatenate([ch, widen(rh)], axis=1)
            rests = jnp.concatenate([cl, widen(rl)], axis=1)
            bracket = 1.5 * eye - 0.5 * prod
            cr[j] = dot(lhs3(bracket), jnp.concatenate([firsts, firsts, rests], axis=0))
        return carry

    fresh = []
    for j in range(4):
        arrived(yrecv.at[j], py_s, py_r.at[j])
        baux[j] = (baux[j] + yrecv[j]) * w_over[j : j + 1]
        fresh.append(dot(lhs3(baux[j] + (aux_p[0, j] - dss[j]) + us[j]), x_rhs[j]))
    for j in range(4):
        tall = fresh[j] + talls[j]
        evos[j] = fresh[j]
        talls[j] = tall
        part = narrow(gram_of([tall], [tall]))
        gsend[2 * j] = part[0:32]
        gsend[2 * j + 1] = part[32:64]
    scatter(gsend, grecv, g1_s, g1_r)
    for j in range(4):
        at_s[0, j] = (evos[j] + dss[j]) * a_rows[j : j + 1]
    halo_send(at_s.at[0], hal_t.at[0], ht_s, ht_r.at[0])
    from_chan(grecv, g1_s, g1_r)
    spread(gall, g2_s, g2_r, total_of(grecv))
    smooth(0)
    delta_t = transposed(delta)
    from_chan(gall, g2_s, g2_r)
    grams = [jnp.concatenate([gall[2 * j], gall[2 * j + 1]], axis=0) for j in range(4)]

    for it in range(INNER):
        last = it == INNER - 1
        delta_l = lhs3(delta)
        delta_r = rhs3(delta_t)
        lefts = [dot(delta_l, rhs3(grams[j])) for j in range(4)]
        traces = [half_sums(jnp.sum(lefts[j] * delta, axis=0, keepdims=True)) + EPS_TRACE for j in range(4)]
        scales = [1.0 / jnp.sqrt(traces[j]) for j in range(4)]
        normals = [dot(lhs3(lefts[j]), delta_r) for j in range(4)]
        curs, brackets = [], []
        for j in range(4):
            left_s[j] = lefts[j]
            curs.append(normals[j] * (1.0 / traces[j]))
            brackets.append(1.5 * eye - 0.5 * curs[j])
        firsts = [mm(brackets[j], curs[j]) for j in range(4)]
        for j in range(4):
            cr[j, :, 0:128] = firsts[j]
            cr[j, :, 128:256] = brackets[j]

        if it == 0:
            lax.fori_loop(0, 3, polar, 0)
            gather_sums(0)
            lax.fori_loop(0, POLAR - 5, polar, 0)
        elif it == 1:
            lax.fori_loop(0, 2, polar, 0)
            smooth(1)
            lax.fori_loop(0, POLAR - 4, polar, 0)
        else:
            lax.fori_loop(0, POLAR - 2, polar, 0)
        boths = [cr[j] for j in range(4)]
        prods = [mm(boths[j][:, 128:256], boths[j][:, 0:128]) for j in range(4)]
        roots = [mm(1.5 * eye - 0.5 * prods[j], boths[j][:, 128:256]) for j in range(4)]
        parts = [mm(roots[j], left_s[j]) * scales[j] for j in range(4)]
        for j in range(4):
            x_s[j] = roots[j]
        part = (parts[0] + parts[1]) + (parts[2] + parts[3])
        part = part + swap(part)
        packed = jnp.where(low, part[0:32], part[32:64])
        for q in range(4):
            qsend[it * 4 + q] = packed[8 * q : 8 * q + 8]
        for d in range(1, 4):
            to = lax.rem(quad + d, 4)
            send(qsend.at[it * 4 + to], qrecv.at[it, quad], q1_s, q1_r.at[it], quad_dev(to))
        qrecv[it, quad] = qsend[it * 4 + quad]
        if it == 1:
            gather_sums(1)
        delta_tl = lhs3(delta_t)
        for j in range(4):
            root = x_s[j]
            k_l[j] = lhs3(dot(delta_tl, rhs3(root)) * scales[j])
            if not last:
                gram_l[j] = lhs3(grams[j])
        arrived(qrecv.at[it, pl.ds(0, 3)], q1_s, q1_r.at[it])
        mine = zbuf.at[it * 32 + zz * 4 + quad]
        mine[...] = (qrecv[it, 0] + qrecv[it, 1]) + (qrecv[it, 2] + qrecv[it, 3])
        for d in (4, 3, 5, 2, 6, 1, 7, 0):
            z = lax.rem(zz + d, 8)
            for e in range(4):
                if d + e:
                    q = lax.rem(quad + e, 4)
                    dev = ((q // 2) * 16 + z * 2 + lax.rem(q, 2), chan)
                    send(mine, mine, z_s, z_r.at[it], dev)
        if last:
            for j in range(4):
                evo, tall = rows_of(j)
                talls[j] = tall
                out_o[j] = evo
        if not last:
            from_chan(sall.at[it], s2_s, s2_r.at[it])
            for j in range(4):
                gut = jnp.concatenate([sall[it, 2 * j, 1], sall[it, 2 * j + 1, 1]], axis=0)
                gtu_s[j] = narrow(jnp.concatenate([gut, gut], axis=0).T)
        arrived(zbuf.at[pl.ds(it * 32, 31)], z_s, z_r.at[it])
        packed = []
        for q in range(4):
            total = zbuf[it * 32 + q]
            for z in range(1, 8):
                total = total + zbuf[it * 32 + 4 * z + q]
            packed.append(total * (1.0 / 256.0))
        delta = unpack(jnp.concatenate(packed, axis=0))
        fresh_r = rhs3(delta)

        if last:
            mixers = [dot(k_l[j], fresh_r) for j in range(4)]
            coups = [mm(talls[j], mixers[j]) for j in range(4)]
            for j in range(4):
                out_o[4 + j] = coups[j]
            delta_o[...] = delta[:, 0:64]
        else:
            mixers = [dot(k_l[j], fresh_r) for j in range(4)]
            turns = [dot(lhs3(2.0 * mixers[j] - eye), x_rhs[j]) for j in range(4)]
            for j in range(4):
                mix_s[j, :, 0:128] = rhs3(turns[j])
                mix_s[j, :, 128:256] = rhs3(mixers[j])
            steps = [turns[j] + (eye - mixers[j]) for j in range(4)]
            sides = [gtu_s[j] + 0.5 * dot(gram_l[j], rhs3(steps[j])) for j in range(4)]
            delta_t = transposed(delta)
            if it == 0:
                fresh = [rows_of(j) for j in range(4)]
                for j in range(4):
                    evos[j], talls[j] = fresh[j]
                    at_s[1, j] = (fresh[j][0] + dss[j]) * a_rows[j : j + 1]
            grams = []
            for j in range(4):
                guu = jnp.concatenate([sall[it, 2 * j, 0], sall[it, 2 * j + 1, 0]], axis=0)
                grams.append(guu + narrow(gram_of([steps[j], sides[j]], [sides[j], steps[j]])))
            if it == 0:
                halo_send(at_s.at[1], hal_t.at[1], ht_s, ht_r.at[1])

    for ref, ssem, rsem in (
        (psend.at[pl.ds(0, 3)], px_s, px_r.at[0]),
        (ysend, py_s, py_r.at[0]),
        (fg.at[pl.ds(0, 7)], fg_s, fg_r),
        (gsend.at[pl.ds(0, 7)], g1_s, g1_r),
        (gall.at[pl.ds(0, 7)], g2_s, g2_r),
        (ssend.at[:, pl.ds(0, 7)], s1_s, s1_r.at[0]),
        (sall.at[:, pl.ds(0, 7)], s2_s, s2_r.at[0]),
        (qsend.at[pl.ds(0, 9)], q1_s, q1_r.at[0]),
        (zbuf.at[pl.ds(0, 93)], z_s, z_r.at[0]),
        (hal_a, ha_s, ha_r.at[0]),
        (hal_t, ht_s, ht_r.at[0]),
        (hal_b, hb_s, hb_r),
    ):
        whole(ref, ssem, rsem).wait_send()


def unpair(out_p, delta_p, evo_o, coup_o, delta_o):
    for j in range(4):
        evo, coup = out_p[j], out_p[4 + j]
        evo_o[j] = evo[:, 0:64]
        evo_o[j + 4] = evo[:, 64:128]
        coup_o[j] = coup[:, 0:64]
        coup_o[j + 4] = coup[:, 64:128]
    delta_o[...] = delta_p[...]


def body(data, order, chan_factor, slice_weights, smooth_aux, coupled, smooth_dual, coupling_dual, delta):
    vm = pltpu.VMEM
    dma = pltpu.SemaphoreType.DMA
    rows = (4, 48, 128)
    anyspace = pl.BlockSpec(memory_space=pl.ANY)
    vspace = pl.BlockSpec(memory_space=pltpu.VMEM)
    paired, delta_out = pl.pallas_call(
        kernel,
        out_shape=(jax.ShapeDtypeStruct((8, 48, 128), F32), jax.ShapeDtypeStruct((64, 64), F32)),
        in_specs=[pl.BlockSpec(memory_space=pltpu.SMEM)] + [anyspace] * 8,
        out_specs=(vspace, vspace),
        scratch_shapes=[
            vm((8, 384, 128), BF16), vm((64, 128), BF16), vm((8, 64), F32), vm((4, 8, 48, 64), F32), vm((64, 64), F32),
            vm((4, 4, 2, 48, 128), F32), vm((4, 4, 2, 48, 128), F32), vm(rows, F32), vm(rows, F32),
            vm((8, 32, 128), F32), vm((4, 64, 128), F32), vm((4, 64, 384), BF16), vm((4, 384, 128), BF16),
            vm((4, 64, 256), F32), vm((4, 64, 128), F32), vm((4, 64, 384), BF16),
            vm((4, 64, 384), BF16), vm((4, 64, 128), F32),
            vm((8, 32, 128), F32), vm((8, 32, 128), F32), vm((8, 32, 128), F32),
            vm((2, 8, 2, 32, 128), F32), vm((2, 8, 2, 32, 128), F32), vm((2, 8, 2, 32, 128), F32),
            vm((12, 8, 128), F32), vm((3, 4, 8, 128), F32), vm((96, 8, 128), F32),
            vm((2,) + rows, F32), vm(rows, F32), vm(rows, F32), vm(rows, F32), vm(rows, F32), vm((4, 384, 256), BF16),
            vm((2,) + rows, F32), vm(rows, F32),
            vm((2, 2) + rows, F32), vm((2, 2) + rows, F32), vm((8, 128), F32), vm((2, 8, 128), F32),
            dma((5,)), dma, dma((4,)), dma, dma((4,)), dma, dma, dma, dma, dma, dma, dma, dma((2,)), dma, dma((2,)),
            dma, dma((3,)), dma, dma((3,)), dma, dma((2,)), dma, dma((2,)), dma, dma,
        ],
        compiler_params=pltpu.CompilerParams(
            collective_id=0, has_side_effects=True, vmem_limit_bytes=60 * 1024 * 1024
        ),
    )(order, data, chan_factor.T, slice_weights, smooth_aux, coupled, smooth_dual, coupling_dual, delta)
    return pl.pallas_call(
        unpair,
        out_shape=(
            jax.ShapeDtypeStruct((8, 48, 64), F32),
            jax.ShapeDtypeStruct((8, 48, 64), F32),
            jax.ShapeDtypeStruct((64, 64), F32),
        ),
        in_specs=[vspace, vspace],
        out_specs=(vspace, vspace, vspace),
    )(paired, delta_out)


def solution(mesh):
    return jax.shard_map(
        body,
        mesh=mesh,
        in_specs=(
            P("cuts", None, "chan"),
            P("cuts"),
            P("chan", None),
            P("cuts", None),
            P("cuts", "chan", None),
            P("cuts", "chan", None),
            P("cuts", "chan", None),
            P("cuts", "chan", None),
            P(),
        ),
        out_specs=(P("cuts", "chan", None), P("cuts", "chan", None), P()),
        check_vma=False,
    )
```

```python
import jax
import jax.numpy as jnp
from jax import lax
from jax.experimental import pallas as pl
from jax.experimental.pallas import tpu as pltpu
from jax.sharding import PartitionSpec as P

INNER = 3
POLAR = 8
NEWTON = 7
FAR_FIRST = (6, 2, 5, 3, 4, 7, 1)
EPS_TRACE = 1e-06
F32 = jnp.float32
MESH = pl.DeviceIdType.MESH
CHEB_A = 0.1328125 / 1.2578125
CHEB_B = -1.0 / (512.0 * 1.2578125)


BF16 = jnp.bfloat16


def split(a):
    high = a.astype(BF16)
    return high, (a - high.astype(F32)).astype(BF16)


def lhs3(a):
    high, rest = split(a)
    return jnp.concatenate([high, rest, high], axis=1)


def dot(a, b):
    return jnp.dot(a, b, preferred_element_type=F32)


def gram_of(a, b):
    left, right = [], []
    for p, q in zip(a, b):
        ph, pl_ = split(p)
        qh, ql = split(q)
        left += [ph, pl_, ph]
        right += [qh, qh, ql]
    return lax.dot_general(
        jnp.concatenate(left, axis=0), jnp.concatenate(right, axis=0), (((0,), (0,)), ((), ())),
        preferred_element_type=F32,
    )


def kernel(
    order, data_h, fac_h, w_h, aux_h, coup_h, ds_h, dc_h, delta_h,
    out_o, delta_o,
    data_v, fac_v, w_v, rows_v, delta_v,
    psend, precv, ysend, yrecv, fg, x_s, sys_s, x_rhs, cr, left_s, k_l, gram_l, gtu_s,
    gsend, grecv, gall, ssend, srecv, sall, qsend, qrecv, zbuf,
    aux_p, dss, talls, evos, us, mix_s, at_s, baux, hal_a, hal_t, bsend, hal_b,
    load_sem, px_s, px_r, py_s, py_r, fg_s, fg_r, g1_s, g1_r, g2_s, g2_r, s1_s, s1_r, s2_s, s2_r,
    q1_s, q1_r, z_s, z_r, ha_s, ha_r, ht_s, ht_r, hb_s, hb_r,
):
    cuts = lax.axis_index("cuts")
    chan = lax.axis_index("chan")
    core = lax.rem(cuts, 2)
    zz = lax.rem(cuts // 2, 8)
    ylo = cuts // 16
    quad = ylo * 2 + core
    xx = lax.rem(chan, 4)
    yhi = chan // 4
    left_id = lax.rem(cuts + 31, 32)
    right_id = lax.rem(cuts + 1, 32)

    def z_dev(z):
        return (ylo * 16 + z * 2 + core, chan)

    def quad_dev(q):
        return ((q // 2) * 16 + zz * 2 + lax.rem(q, 2), chan)

    def send(src, dst, ssem, rsem, dev):
        pltpu.make_async_remote_copy(
            src_ref=src, dst_ref=dst, send_sem=ssem, recv_sem=rsem, device_id=dev, device_id_type=MESH
        ).start()

    def whole(ref, ssem, rsem):
        return pltpu.make_async_remote_copy(
            src_ref=ref, dst_ref=ref, send_sem=ssem, recv_sem=rsem, device_id=(left_id, chan), device_id_type=MESH
        )

    def arrived(ref, ssem, rsem):
        whole(ref, ssem, rsem).wait_recv()

    def load(src, dst, n):
        return pltpu.make_async_copy(src, dst, load_sem.at[n])

    load(fac_h, fac_v, 0).start()
    load(data_h, data_v, 1).start()
    load(w_h, w_v, 2).start()
    for n, src in enumerate((aux_h, coup_h, ds_h, dc_h)):
        load(src, rows_v.at[n], 3).start()
    load(delta_h, delta_v, 4).start()

    barrier = pltpu.get_barrier_semaphore()
    greet = [(cuts, lax.rem(chan + d, 8)) for d in range(1, 8)]
    greet += [(lax.rem(cuts + d, 32), chan) for d in range(1, 32)]
    for dev in greet:
        pl.semaphore_signal(barrier, inc=1, device_id=dev, device_id_type=MESH)

    lane = lax.broadcasted_iota(jnp.int32, (1, 128), 1)
    low = lane < 64
    high = lane >= 64
    row_i = lax.broadcasted_iota(jnp.int32, (64, 128), 0)
    col_i = lax.broadcasted_iota(jnp.int32, (64, 128), 1)
    eye_b = row_i == lax.rem(col_i, 64)
    eye = eye_b.astype(F32)
    low16 = low.astype(F32).astype(BF16)
    high16 = high.astype(F32).astype(BF16)

    def swap(v):
        return pltpu.roll(v, 64, 1)

    def widen(v):
        return jnp.concatenate([v * low16, v * high16], axis=0)

    def rhs3(a):
        first, rest = split(a)
        first, rest = widen(first), widen(rest)
        return jnp.concatenate([first, first, rest], axis=0)

    def mm(a, b):
        return dot(lhs3(a), rhs3(b))

    def narrow(t):
        return jnp.where(low, t[0:64], t[64:128])

    def unpack(p):
        q = swap(p)
        return jnp.concatenate([jnp.where(low, p, q), jnp.where(low, q, p)], axis=0)

    def transposed(c):
        return jnp.concatenate([c, c], axis=0).T[0:64]

    def half_sums(v):
        zero = jnp.zeros_like(v)
        lo = jnp.sum(jnp.where(low, v, zero), axis=1, keepdims=True)
        hi = jnp.sum(jnp.where(low, zero, v), axis=1, keepdims=True)
        return jnp.where(low, lo, hi)

    load(fac_h, fac_v, 0).wait()
    fac = fac_v[...]
    nt = (((1,), (1,)), ((), ()))
    partial_gram = lax.dot_general(fac, fac, nt, preferred_element_type=F32)
    fg[chan] = jnp.concatenate([partial_gram[0:32], partial_gram[32:64]], axis=1)
    zero_fac = jnp.zeros_like(fac)
    fac2 = jnp.concatenate(
        [jnp.concatenate([fac, zero_fac], axis=1), jnp.concatenate([zero_fac, fac], axis=1)], axis=0
    )
    load(data_h, data_v, 1).wait()
    for j in range(4):
        first = data_v[lax.rem(order[j], 8)]
        second = data_v[lax.rem(order[j + 4], 8)]
        out = lax.dot_general(jnp.concatenate([first, second], axis=1), fac2, nt, preferred_element_type=F32)
        for c in range(8):
            psend[j, c % 4, c // 4] = out[48 * c : 48 * c + 48]
    pl.semaphore_wait(barrier, len(greet))
    for d in FAR_FIRST:
        peer = lax.rem(chan + d, 8)
        send(fg.at[chan], fg.at[chan], fg_s, fg_r, (cuts, peer))
    for j in range(4):
        for d in (2, 1, 3):
            to = lax.rem(xx + d, 4)
            send(psend.at[j, to], precv.at[j, xx], px_s, px_r.at[j], (cuts, yhi * 4 + to))

    load(w_h, w_v, 2).wait()
    load(rows_v, rows_v, 3).wait()
    load(delta_h, delta_v, 4).wait()

    def pair(n, j):
        return jnp.concatenate([rows_v[n, j], rows_v[n, j + 4]], axis=1)

    for j in range(4):
        aux_p[0, j] = pair(0, j)
        dss[j] = pair(2, j)
        dual = pair(3, j)
        talls[j] = dual
        us[j] = pair(1, j) - dual

    def halo_send(src, dst, ssem, rsem):
        send(src, dst.at[0], ssem, rsem, (right_id, chan))
        send(src, dst.at[1], ssem, rsem, (left_id, chan))

    halo_send(aux_p.at[0], hal_a.at[0], ha_s, ha_r.at[0])

    arrived(fg.at[pl.ds(0, 7)], fg_s, fg_r)
    gram_sum = fg[0]
    for c in range(1, 8):
        gram_sum = gram_sum + fg[c]
    gram2 = unpack(gram_sum)
    w = w_v[...]
    w2 = jnp.concatenate([w[0:4], w[4:8]], axis=1)
    diag_row = jnp.sum(jnp.where(eye_b, gram2, 0.0), axis=0, keepdims=True)
    rho = half_sums(w2 * w2 * diag_row) * (1.0 / 64.0)
    w_over = w2 / rho
    b_rows = 2.0 / (rho + 4.0)
    a_rows = rho / (rho + 4.0)
    bsend[0:4] = b_rows
    bsend[4:8] = b_rows
    halo_send(bsend, hal_b, hb_s, hb_r)
    for j in range(4):
        w_col = half_sums(jnp.where(eye_b, w2[j : j + 1], 0.0))
        system = gram2 * w_col * w_over[j : j + 1] + 2.0 * eye
        sys_s[j] = lhs3(system)
        x_s[j] = CHEB_A * eye + CHEB_B * system

    def newton(step, carry):
        xs = [x_s[j] for j in range(4)]
        gaps = [2.0 * eye - dot(sys_s[j], rhs3(xs[j])) for j in range(4)]
        fresh = [mm(xs[j], gaps[j]) for j in range(4)]
        for j in range(4):
            x_s[j] = fresh[j]
        return carry

    def forward(j):
        arrived(precv.at[j, pl.ds(0, 3)], px_s, px_r.at[j])
        total = psend[j, xx, 1 - yhi]
        for d in range(1, 4):
            total = total + precv[j, lax.rem(xx + d, 4), 1 - yhi]
        ysend[j] = total
        send(ysend.at[j], yrecv.at[j], py_s, py_r.at[j], (cuts, (1 - yhi) * 4 + xx))
        total = psend[j, xx, yhi]
        for d in range(1, 4):
            total = total + precv[j, lax.rem(xx + d, 4), yhi]
        baux[j] = total

    lax.fori_loop(0, 2, newton, 0)
    forward(0)
    lax.fori_loop(0, 3, newton, 0)
    forward(1)
    lax.fori_loop(0, NEWTON - 5, newton, 0)
    forward(2)
    for j in range(4):
        x_rhs[j] = rhs3(x_s[j])
    forward(3)

    delta_in = delta_v[...]
    delta = jnp.concatenate([delta_in, delta_in], axis=1)

    def spread(buf, ssem, rsem, own):
        buf[chan] = own
        for d in FAR_FIRST:
            send(buf.at[chan], buf.at[chan], ssem, rsem, (cuts, lax.rem(chan + d, 8)))

    def scatter(src, dst, ssem, rsem):
        for d in FAR_FIRST:
            peer = lax.rem(chan + d, 8)
            send(src.at[peer], dst.at[chan], ssem, rsem, (cuts, peer))
        dst[chan] = src[chan]

    def from_chan(buf, ssem, rsem):
        arrived(buf.at[pl.ds(0, 7)], ssem, rsem)

    def total_of(buf):
        total = buf[0]
        for c in range(1, 8):
            total = total + buf[c]
        return total

    def smooth(it):
        arrived(hal_a.at[it], ha_s, ha_r.at[it])
        arrived(hal_t.at[it], ht_s, ht_r.at[it])
        if it == 0:
            arrived(hal_b, hb_s, hb_r)
        vals, tars, bs = [], [], []
        for p in range(4):
            vals.append(jnp.where(low, swap(hal_a[it, 0, p]), aux_p[it, p]))
            tars.append(jnp.where(low, swap(hal_t[it, 0, p]), at_s[it, p]))
            bs.append(jnp.where(low, swap(hal_b[0, p : p + 1]), bsend[p : p + 1]))
        for p in range(4):
            vals.append(jnp.where(low, aux_p[it, p], swap(hal_a[it, 1, p])))
            tars.append(jnp.where(low, at_s[it, p], swap(hal_t[it, 1, p])))
            bs.append(jnp.where(low, bsend[p : p + 1], swap(hal_b[1, p : p + 1])))
        for sweep in range(4):
            fresh = []
            for p in range(8):
                before = vals[p - 1] if p > 0 else swap(vals[7])
                after = vals[p + 1] if p < 7 else swap(vals[0])
                fresh.append(tars[p] + bs[p] * (before + after))
            vals = fresh
        for j in range(4):
            aux = jnp.where(low, vals[4 + j], vals[j])
            dual = dss[j] + evos[j] - aux
            if it == 0:
                aux_p[1, j] = aux
            dss[j] = dual
            us[j] = dot(lhs3(baux[j] + (aux - dual)), x_rhs[j])
        if it == 0:
            halo_send(aux_p.at[1], hal_a.at[1], ha_s, ha_r.at[1])
        for j in range(4):
            u, tall = us[j], talls[j]
            sums = gram_of([u], [jnp.concatenate([u, tall], axis=1)])
            guu, gut = narrow(sums[:, 0:128]), narrow(sums[:, 128:256])
            for h in range(2):
                ssend[it, 2 * j + h, 0] = guu[32 * h : 32 * h + 32]
                ssend[it, 2 * j + h, 1] = gut[32 * h : 32 * h + 32]
        scatter(ssend.at[it], srecv.at[it], s1_s, s1_r.at[it])

    def gather_sums(it):
        from_chan(srecv.at[it], s1_s, s1_r.at[it])
        spread(sall.at[it], s2_s, s2_r.at[it], total_of(srecv.at[it]))

    def rows_of(j):
        tall = talls[j]
        both = dot(lhs3(tall), mix_s[j])
        evo = us[j] + both[:, 0:128]
        return evo, evo + (tall - both[:, 128:256])

    def polar(step, carry):
        for j in range(4):
            both = cr[j]
            root = both[:, 128:256]
            ch, cl = split(both[:, 0:128])
            rh, rl = split(root)
            ch, cl = widen(ch), widen(cl)
            prod = dot(lhs3(root), jnp.concatenate([ch, ch, cl], axis=0))
            firsts = jnp.concatenate([ch, widen(rh)], axis=1)
            rests = jnp.concatenate([cl, widen(rl)], axis=1)
            bracket = 1.5 * eye - 0.5 * prod
            cr[j] = dot(lhs3(bracket), jnp.concatenate([firsts, firsts, rests], axis=0))
        return carry

    fresh = []
    for j in range(4):
        arrived(yrecv.at[j], py_s, py_r.at[j])
        baux[j] = (baux[j] + yrecv[j]) * w_over[j : j + 1]
        fresh.append(dot(lhs3(baux[j] + (aux_p[0, j] - dss[j]) + us[j]), x_rhs[j]))
    for j in range(4):
        tall = fresh[j] + talls[j]
        evos[j] = fresh[j]
        talls[j] = tall
        part = narrow(gram_of([tall], [tall]))
        gsend[2 * j] = part[0:32]
        gsend[2 * j + 1] = part[32:64]
    scatter(gsend, grecv, g1_s, g1_r)
    for j in range(4):
        at_s[0, j] = (evos[j] + dss[j]) * a_rows[j : j + 1]
    halo_send(at_s.at[0], hal_t.at[0], ht_s, ht_r.at[0])
    from_chan(grecv, g1_s, g1_r)
    spread(gall, g2_s, g2_r, total_of(grecv))
    smooth(0)
    delta_t = transposed(delta)
    from_chan(gall, g2_s, g2_r)
    grams = [jnp.concatenate([gall[2 * j], gall[2 * j + 1]], axis=0) for j in range(4)]

    for it in range(INNER):
        last = it == INNER - 1
        delta_l = lhs3(delta)
        delta_r = rhs3(delta_t)
        lefts = [dot(delta_l, rhs3(grams[j])) for j in range(4)]
        traces = [half_sums(jnp.sum(lefts[j] * delta, axis=0, keepdims=True)) + EPS_TRACE for j in range(4)]
        scales = [1.0 / jnp.sqrt(traces[j]) for j in range(4)]
        normals = [dot(lhs3(lefts[j]), delta_r) for j in range(4)]
        curs, brackets = [], []
        for j in range(4):
            left_s[j] = lefts[j]
            curs.append(normals[j] * (1.0 / traces[j]))
            brackets.append(1.5 * eye - 0.5 * curs[j])
        firsts = [mm(brackets[j], curs[j]) for j in range(4)]
        for j in range(4):
            cr[j, :, 0:128] = firsts[j]
            cr[j, :, 128:256] = brackets[j]

        if it == 0:
            lax.fori_loop(0, 3, polar, 0)
            gather_sums(0)
            lax.fori_loop(0, POLAR - 5, polar, 0)
        elif it == 1:
            lax.fori_loop(0, 2, polar, 0)
            smooth(1)
            lax.fori_loop(0, POLAR - 4, polar, 0)
        else:
            lax.fori_loop(0, POLAR - 2, polar, 0)
        boths = [cr[j] for j in range(4)]
        prods = [mm(boths[j][:, 128:256], boths[j][:, 0:128]) for j in range(4)]
        roots = [mm(1.5 * eye - 0.5 * prods[j], boths[j][:, 128:256]) for j in range(4)]
        parts = [mm(roots[j], left_s[j]) * scales[j] for j in range(4)]
        for j in range(4):
            x_s[j] = roots[j]
        part = (parts[0] + parts[1]) + (parts[2] + parts[3])
        part = part + swap(part)
        packed = jnp.where(low, part[0:32], part[32:64])
        for q in range(4):
            qsend[it * 4 + q] = packed[8 * q : 8 * q + 8]
        for d in range(1, 4):
            to = lax.rem(quad + d, 4)
            send(qsend.at[it * 4 + to], qrecv.at[it, quad], q1_s, q1_r.at[it], quad_dev(to))
        qrecv[it, quad] = qsend[it * 4 + quad]
        if it == 1:
            gather_sums(1)
        delta_tl = lhs3(delta_t)
        for j in range(4):
            root = x_s[j]
            k_l[j] = lhs3(dot(delta_tl, rhs3(root)) * scales[j])
            if not last:
                gram_l[j] = lhs3(grams[j])
        arrived(qrecv.at[it, pl.ds(0, 3)], q1_s, q1_r.at[it])
        mine = zbuf.at[it * 32 + zz * 4 + quad]
        mine[...] = (qrecv[it, 0] + qrecv[it, 1]) + (qrecv[it, 2] + qrecv[it, 3])
        for d in (4, 3, 5, 2, 6, 1, 7, 0):
            z = lax.rem(zz + d, 8)
            for e in range(4):
                if d + e:
                    q = lax.rem(quad + e, 4)
                    dev = ((q // 2) * 16 + z * 2 + lax.rem(q, 2), chan)
                    send(mine, mine, z_s, z_r.at[it], dev)
        if last:
            for j in range(4):
                evo, tall = rows_of(j)
                talls[j] = tall
                out_o[j] = evo
        if not last:
            from_chan(sall.at[it], s2_s, s2_r.at[it])
            for j in range(4):
                gut = jnp.concatenate([sall[it, 2 * j, 1], sall[it, 2 * j + 1, 1]], axis=0)
                gtu_s[j] = narrow(jnp.concatenate([gut, gut], axis=0).T)
        arrived(zbuf.at[pl.ds(it * 32, 31)], z_s, z_r.at[it])
        packed = []
        for q in range(4):
            total = zbuf[it * 32 + q]
            for z in range(1, 8):
                total = total + zbuf[it * 32 + 4 * z + q]
            packed.append(total * (1.0 / 256.0))
        delta = unpack(jnp.concatenate(packed, axis=0))
        fresh_r = rhs3(delta)

        if last:
            mixers = [dot(k_l[j], fresh_r) for j in range(4)]
            coups = [mm(talls[j], mixers[j]) for j in range(4)]
            for j in range(4):
                out_o[4 + j] = coups[j]
            delta_o[...] = delta[:, 0:64]
        else:
            mixers = [dot(k_l[j], fresh_r) for j in range(4)]
            turns = [dot(lhs3(2.0 * mixers[j] - eye), x_rhs[j]) for j in range(4)]
            for j in range(4):
                mix_s[j, :, 0:128] = rhs3(turns[j])
                mix_s[j, :, 128:256] = rhs3(mixers[j])
            steps = [turns[j] + (eye - mixers[j]) for j in range(4)]
            sides = [gtu_s[j] + 0.5 * dot(gram_l[j], rhs3(steps[j])) for j in range(4)]
            delta_t = transposed(delta)
            if it == 0:
                fresh = [rows_of(j) for j in range(4)]
                for j in range(4):
                    evos[j], talls[j] = fresh[j]
                    at_s[1, j] = (fresh[j][0] + dss[j]) * a_rows[j : j + 1]
            grams = []
            for j in range(4):
                guu = jnp.concatenate([sall[it, 2 * j, 0], sall[it, 2 * j + 1, 0]], axis=0)
                grams.append(guu + narrow(gram_of([steps[j], sides[j]], [sides[j], steps[j]])))
            if it == 0:
                halo_send(at_s.at[1], hal_t.at[1], ht_s, ht_r.at[1])

    for ref, ssem, rsem in (
        (psend.at[pl.ds(0, 3)], px_s, px_r.at[0]),
        (ysend, py_s, py_r.at[0]),
        (fg.at[pl.ds(0, 7)], fg_s, fg_r),
        (gsend.at[pl.ds(0, 7)], g1_s, g1_r),
        (gall.at[pl.ds(0, 7)], g2_s, g2_r),
        (ssend.at[:, pl.ds(0, 7)], s1_s, s1_r.at[0]),
        (sall.at[:, pl.ds(0, 7)], s2_s, s2_r.at[0]),
        (qsend.at[pl.ds(0, 9)], q1_s, q1_r.at[0]),
        (zbuf.at[pl.ds(0, 93)], z_s, z_r.at[0]),
        (hal_a, ha_s, ha_r.at[0]),
        (hal_t, ht_s, ht_r.at[0]),
        (hal_b, hb_s, hb_r),
    ):
        whole(ref, ssem, rsem).wait_send()


def unpair(out_p, delta_p, evo_o, coup_o, delta_o):
    for j in range(4):
        evo, coup = out_p[j], out_p[4 + j]
        evo_o[j] = evo[:, 0:64]
        evo_o[j + 4] = evo[:, 64:128]
        coup_o[j] = coup[:, 0:64]
        coup_o[j + 4] = coup[:, 64:128]
    delta_o[...] = delta_p[...]


def body(data, order, chan_factor, slice_weights, smooth_aux, coupled, smooth_dual, coupling_dual, delta):
    vm = pltpu.VMEM
    dma = pltpu.SemaphoreType.DMA
    rows = (4, 48, 128)
    anyspace = pl.BlockSpec(memory_space=pl.ANY)
    vspace = pl.BlockSpec(memory_space=pltpu.VMEM)
    paired, delta_out = pl.pallas_call(
        kernel,
        out_shape=(jax.ShapeDtypeStruct((8, 48, 128), F32), jax.ShapeDtypeStruct((64, 64), F32)),
        in_specs=[pl.BlockSpec(memory_space=pltpu.SMEM)] + [anyspace] * 8,
        out_specs=(vspace, vspace),
        scratch_shapes=[
            vm((8, 384, 128), BF16), vm((64, 128), BF16), vm((8, 64), F32), vm((4, 8, 48, 64), F32), vm((64, 64), F32),
            vm((4, 4, 2, 48, 128), F32), vm((4, 4, 2, 48, 128), F32), vm(rows, F32), vm(rows, F32),
            vm((8, 32, 128), F32), vm((4, 64, 128), F32), vm((4, 64, 384), BF16), vm((4, 384, 128), BF16),
            vm((4, 64, 256), F32), vm((4, 64, 128), F32), vm((4, 64, 384), BF16),
            vm((4, 64, 384), BF16), vm((4, 64, 128), F32),
            vm((8, 32, 128), F32), vm((8, 32, 128), F32), vm((8, 32, 128), F32),
            vm((2, 8, 2, 32, 128), F32), vm((2, 8, 2, 32, 128), F32), vm((2, 8, 2, 32, 128), F32),
            vm((12, 8, 128), F32), vm((3, 4, 8, 128), F32), vm((96, 8, 128), F32),
            vm((2,) + rows, F32), vm(rows, F32), vm(rows, F32), vm(rows, F32), vm(rows, F32), vm((4, 384, 256), BF16),
            vm((2,) + rows, F32), vm(rows, F32),
            vm((2, 2) + rows, F32), vm((2, 2) + rows, F32), vm((8, 128), F32), vm((2, 8, 128), F32),
            dma((5,)), dma, dma((4,)), dma, dma((4,)), dma, dma, dma, dma, dma, dma, dma, dma((2,)), dma, dma((2,)),
            dma, dma((3,)), dma, dma((3,)), dma, dma((2,)), dma, dma((2,)), dma, dma,
        ],
        compiler_params=pltpu.CompilerParams(
            collective_id=0, has_side_effects=True, vmem_limit_bytes=60 * 1024 * 1024
        ),
    )(order, data, chan_factor.T, slice_weights, smooth_aux, coupled, smooth_dual, coupling_dual, delta)
    return pl.pallas_call(
        unpair,
        out_shape=(
            jax.ShapeDtypeStruct((8, 48, 64), F32),
            jax.ShapeDtypeStruct((8, 48, 64), F32),
            jax.ShapeDtypeStruct((64, 64), F32),
        ),
        in_specs=[vspace, vspace],
        out_specs=(vspace, vspace, vspace),
    )(paired, delta_out)


def solution(mesh):
    return jax.shard_map(
        body,
        mesh=mesh,
        in_specs=(
            P("cuts", None, "chan"),
            P("cuts"),
            P("chan", None),
            P("cuts", None),
            P("cuts", "chan", None),
            P("cuts", "chan", None),
            P("cuts", "chan", None),
            P("cuts", "chan", None),
            P(),
        ),
        out_specs=(P("cuts", "chan", None), P("cuts", "chan", None), P()),
        check_vma=False,
    )
```
